32 devices in a mesh: member: 2 (over x), tx: 4 (over y, core), ty: 4 (over z).
Axes of the slice: x: 2, y: 2, z: 4, core: 2. Of those that a mesh axis runs over, the one named last changes fastest.
Arguments:
- state: float32 [1024, 128, 128], P(('member', 'tx'), 'ty'), parts along dimension 0, may hold values from -6 to 6
- courant: bfloat16 [1024, 128, 128], P(('member', 'tx'), 'ty'), parts along dimension 0, may hold values from -0.3984375 to 0.3984375
- diffusion: float32 [1024, 128], P(('member', 'tx'), 'ty'), parts along dimension 0, may hold values from 0.02 to 0.2
- conv_mask: int32 [1024, 128], P(('member', 'tx'), 'ty'), parts along dimension 0, may hold values from 0 to 1, as said below
- w_in: bfloat16 [128, 1024], replicated, may hold values from -0.5 to 0.5
- w_hidden: bfloat16 [3, 1024, 1024], replicated, may hold values from -0.1875 to 0.1875
- w_out: bfloat16 [1024, 128], replicated, may hold values from -0.1875 to 0.1875
Outputs:
- state_out: float32 [1024, 128, 128], P(('member', 'tx'), 'ty'), parts along dimension 0
The draws below stay inside these ranges and needn't reach their ends.
There are 2 independent parts, one for each index of `member`. The reference program is written for one: setup_inputs(seed, part) draws one part's arguments, and reference() takes and returns one part's arrays. A program takes and returns all parts, laid end to end along the dimension named above; an argument that names none is the same for every part. Nothing has to cross between parts.
Inputs may be any that keep to these rules, and one draw needn't show every extreme that they name: `conv_mask`: A tile is one device's 128 x 32 columns. A tile's used blocks are ceil(its flagged columns / 32); at most 64, reached by some tile; over a member's tiles they sum to exactly 528.
All inputs are finite; a program needn't handle non-finite values.
Results may differ from the reference program's by a relative error of at most 0.00033.
Values may be sent and summed in bfloat16 or wider, within the bound.
A program may use at most 64 MiB of HBM per device.

```python
import math
import jax
import jax.numpy as jnp
from jax import lax

CLON = 128
CLAT = 32
LEV = 64
CH = 128
HID = 1024
LAYERS = 5
BLK = 32
NBLK = 64
MEAN = 33
NLON = 512
NLAT = 128
N_TX = 4
N_TY = 4


def tile_order(sub_key):
    return jax.random.permutation(sub_key, CLON * CLAT)


def draw_conv_mask(key, part):
    tile_count = N_TX * N_TY
    half_count = tile_count // 2
    key_pair = jax.random.fold_in(key, 3)
    key_perm = jax.random.fold_in(key, 5)
    key_trim = jax.random.fold_in(key, 7)
    key_rank = jax.random.fold_in(key, 11)
    first = jax.random.randint(key_pair, (half_count,), 2, 2 * MEAN - 1)
    first = first.at[0].set(NBLK)
    loads = jnp.concatenate([first, 2 * MEAN - first])
    loads = jax.random.permutation(key_perm, loads)
    trimmed = jax.random.randint(key_trim, (tile_count,), 0, BLK)
    trimmed = jnp.where(loads == NBLK, 0, trimmed)
    flagged = loads * BLK - trimmed
    ranks = jax.vmap(tile_order)(jax.random.split(key_rank, tile_count))
    marks = (ranks < flagged[:, None]).astype(jnp.int32)
    marks = marks.reshape(N_TX, N_TY, CLON, CLAT).transpose(0, 2, 1, 3)
    return marks.reshape(N_TX * CLON, N_TY * CLAT)


def block_scale(stream_key, extent, shards, least, largest):
    def one(position, shards_of):
        steps = jax.random.uniform(jax.random.fold_in(jax.random.fold_in(stream_key, 6), position), (shards_of,), jnp.float32, least / len(shards), largest / len(shards))
        return jnp.repeat(jnp.exp(steps), extent[position] // shards_of).reshape((-1,) + (1,) * (len(extent) - position - 1))

    loudness = one(*shards[0])
    for cut in shards[1:]:
        loudness = loudness * one(*cut)
    return loudness


def noise(own_key, shape, width, most, pieces=(), kind=jnp.bfloat16):
    result = jax.random.normal(own_key, shape, jnp.float32) * width
    if len(pieces) > 0:
        result = block_scale(own_key, shape, pieces, -0.22, 0.18) * result
    return jnp.clip(result, min=-most, max=most).astype(kind)


def setup_inputs(seed: int = 0, part: int = 0) -> dict:
    key_of = jax.random.split(jax.random.key(seed), 8)
    part_splits = jax.random.split(jax.random.fold_in(key_of[7], part), 8)
    return {
        "state": noise(part_splits[0], (NLON, NLAT, CH), 1.0, 6.0, ((0, 4), (1, 4)), jnp.float32),
        "courant": jnp.clip(jax.random.uniform(part_splits[1], (NLON, NLAT, CH), jnp.float32, -0.3984375, 0.3984375) * block_scale(part_splits[1], (NLON, NLAT, CH), ((0, 4), (1, 4)), -0.4, 0.0), -0.3984375, 0.3984375).astype(jnp.bfloat16),
        "diffusion": jnp.clip(jnp.exp(math.log(0.2) - 2.3025851 * jax.random.uniform(part_splits[2], (NLON, NLAT), jnp.float32) ** block_scale(part_splits[2], (NLON, NLAT), ((0, 4), (1, 4)), -0.2, 0.2)), 0.02, 0.2),
        "conv_mask": draw_conv_mask(jax.random.fold_in(jax.random.fold_in(key_of[7], part), 71), part),
        "w_in": noise(key_of[4], (CH, HID), CH ** -0.5, 0.5),
        "w_hidden": noise(key_of[5], (LAYERS - 2, HID, HID), HID ** -0.5, 0.1875),
        "w_out": noise(key_of[6], (HID, CH), HID ** -0.5, 0.1875),
    }


def advance(state, courant, diffusion):
    east = jnp.roll(state, -1, 0)
    west = jnp.roll(state, 1, 0)
    zero_line = jnp.zeros_like(state[:, :1])
    north = jnp.concatenate([state[:, 1:], zero_line], 1)
    south = jnp.concatenate([zero_line, state[:, :-1]], 1)
    wind = courant.astype(jnp.float32)
    along_lon = jnp.concatenate([wind[..., :LEV], wind[..., :LEV]], -1)
    along_lat = jnp.concatenate([wind[..., LEV:], wind[..., LEV:]], -1)
    laplace = east + west + north + south - 4.0 * state
    return state - 0.5 * along_lon * (east - west) - 0.5 * along_lat * (north - south) + diffusion[..., None] * laplace


def closure(inputs, w_in, w_hidden, w_out):
    hidden = jax.nn.silu(jnp.dot(inputs, w_in, preferred_element_type=jnp.float32)).astype(jnp.bfloat16)
    for layer_idx in range(w_hidden.shape[0]):
        hidden = jax.nn.silu(jnp.dot(hidden, w_hidden[layer_idx], preferred_element_type=jnp.float32)).astype(jnp.bfloat16)
    return jnp.dot(hidden, w_out, preferred_element_type=jnp.float32).astype(jnp.bfloat16)


def reference(state, courant, diffusion, conv_mask, w_in, w_hidden, w_out):
    advanced = advance(state, courant, diffusion)
    columns = NLON * NLAT
    capacity = N_TX * N_TY * MEAN * BLK
    flags = conv_mask.reshape(columns).astype(jnp.int32)
    ranks = (jnp.cumsum(flags) - 1).astype(jnp.int32)
    slot_pos = jnp.where(flags == 1, ranks, capacity).astype(jnp.int32)
    features = advanced.reshape(columns, CH).astype(jnp.bfloat16)
    packed = jnp.zeros((capacity, CH), jnp.bfloat16).at[slot_pos].set(features, mode="drop")
    groups = packed.reshape(N_TX * N_TY, MEAN * BLK, CH)
    tendency = lax.map(lambda group: closure(group, w_in, w_hidden, w_out), groups)
    tendency = tendency.reshape(capacity, CH)
    picked = tendency[jnp.minimum(slot_pos, capacity - 1)].astype(jnp.float32)
    added = jnp.where(flags[:, None] == 1, picked, jnp.float32(0.0))
    return (advanced.reshape(columns, CH) + added).reshape(NLON, NLAT, CH)
```

```python
import functools

import jax
import jax.numpy as jnp
from jax import lax
from jax.experimental import pallas as pl
from jax.experimental.pallas import tpu as pltpu
from jax.sharding import PartitionSpec as P

MESH = pl.DeviceIdType.MESH
PAD = 8
PIECES = 4
GRP = 8
CHUNK = 128
ROOM = 55 << 20
TM = 1024
STEP = 256


def onezero(cond):
    return cond.astype(jnp.float32).astype(jnp.bfloat16)


def iota(shape, dim):
    return lax.broadcasted_iota(jnp.int32, shape, dim)


def mm(a, b, dims=((1,), (0,))):
    return lax.dot_general(a, b, (dims, ((), ())), preferred_element_type=jnp.float32)


def advance_kernel(ntx, nty, state_hbm, courant_hbm, diffusion_ref, mask_ref, win_hbm, whid_hbm,
                   adv_ref, win_ref, whid_ref, place_ref, turned_ref, base_ref,
                   tile, wind_v, edge_n, edge_s, halo_n, halo_s, halo_e, halo_w,
                   coef_n, coef_s, coef_e, coef_w, lsem, csem, wsem, ssem, rsem):
    lon, lat, ch = wind_v.shape
    ix, iy = lax.axis_index("tx"), lax.axis_index("ty")
    east, west = lax.rem(ix + 1, ntx), lax.rem(ix + ntx - 1, ntx)
    has_n, has_s = iy < nty - 1, iy > 0
    part = lon // PIECES

    barrier = pltpu.get_barrier_semaphore()
    pl.semaphore_signal(barrier, inc=1, device_id={"tx": east}, device_id_type=MESH)
    pl.semaphore_signal(barrier, inc=1, device_id={"tx": west}, device_id_type=MESH)

    @pl.when(has_n)
    def _():
        pl.semaphore_signal(barrier, inc=1, device_id={"ty": iy + 1}, device_id_type=MESH)

    @pl.when(has_s)
    def _():
        pl.semaphore_signal(barrier, inc=1, device_id={"ty": iy - 1}, device_id_type=MESH)

    loads = [pltpu.make_async_copy(state_hbm.at[pl.ds(k * part, part)],
                                   tile.at[pl.ds(1 + k * part, part), pl.ds(PAD, lat)], lsem.at[k])
             for k in range(PIECES)]
    winds = [pltpu.make_async_copy(courant_hbm.at[pl.ds(k * part, part)],
                                   wind_v.at[pl.ds(k * part, part)], csem.at[k])
             for k in range(PIECES)]
    weights = [pltpu.make_async_copy(win_hbm, win_ref, wsem.at[0]),
               pltpu.make_async_copy(whid_hbm.at[pl.ds(0, 1)], whid_ref, wsem.at[1])]
    for cp in loads + winds + weights:
        cp.start()

    @pl.when(jnp.logical_not(has_n))
    def _():
        halo_n[...] = jnp.zeros_like(halo_n)

    @pl.when(jnp.logical_not(has_s))
    def _():
        halo_s[...] = jnp.zeros_like(halo_s)

    edge = jnp.zeros((lon, 1, ch), jnp.float32)
    tile[pl.ds(1, lon), pl.ds(PAD - 1, 1), :] = edge
    tile[pl.ds(1, lon), pl.ds(PAD + lat, 1), :] = edge
    tile[pl.ds(0, 1), pl.ds(PAD, lat), :] = jnp.zeros((1, lat, ch), jnp.float32)
    tile[pl.ds(lon + 1, 1), pl.ds(PAD, lat), :] = jnp.zeros((1, lat, ch), jnp.float32)

    per = CHUNK // lat
    chunks = lon // per
    flags = mask_ref[...].astype(jnp.float32).astype(jnp.bfloat16)
    spread = onezero(iota((lat, CHUNK), 1) % lat == iota((lat, CHUNK), 0))
    rep = mm(flags, spread, ((0,), (0,)))
    keep = iota((lon, CHUNK), 1) // lat == iota((lon, CHUNK), 0) % per
    rep = jnp.where(keep, rep, 0.0).astype(jnp.bfloat16)
    fold = onezero(iota((chunks, lon), 1) // per == iota((chunks, lon), 0))
    rows = mm(fold, rep)
    rows_b = rows.astype(jnp.bfloat16)
    first, second = iota((CHUNK, CHUNK), 0), iota((CHUNK, CHUNK), 1)
    rank = mm(rows_b, onezero(first < second))
    rank_t = mm(onezero(second < first), rows_b, ((1,), (1,)))
    rows_t = mm(onezero(first == second), rows_b, ((1,), (1,)))
    place_ref[...] = jnp.where(rows > 0.5, rank, -1.0)
    turned_ref[...] = jnp.where(rows_t > 0.5, rank_t, -1.0)
    total = jnp.broadcast_to(jnp.sum(rows, axis=1, keepdims=True), (chunks, CHUNK))
    lower = onezero(iota((chunks, chunks), 1) < iota((chunks, chunks), 0))
    base_ref[...] = mm(lower, total.astype(jnp.bfloat16)).astype(jnp.int32)

    for cp in loads:
        cp.wait()
    edge_n[...] = tile[pl.ds(1, lon), pl.ds(PAD + lat - 1, 1), :]
    edge_s[...] = tile[pl.ds(1, lon), pl.ds(PAD, 1), :]

    pl.semaphore_wait(barrier, 2 + has_n.astype(jnp.int32) + has_s.astype(jnp.int32))

    def send(src, dst, k, dev):
        return pltpu.make_async_remote_copy(
            src_ref=src, dst_ref=dst, send_sem=ssem.at[k], recv_sem=rsem.at[k],
            device_id=dev, device_id_type=MESH)

    to_n = send(edge_n, halo_s, 2, {"ty": iy + 1})
    to_s = send(edge_s, halo_n, 3, {"ty": iy - 1})
    to_e = send(state_hbm.at[pl.ds(lon - 1, 1)], halo_w, 0, {"tx": east})
    to_w = send(state_hbm.at[pl.ds(0, 1)], halo_e, 1, {"tx": west})
    pl.when(has_n)(to_n.start)
    pl.when(has_s)(to_s.start)
    to_e.start()
    to_w.start()

    half = ch // 2
    shape = (GRP, lat, ch)
    lane2 = iota((GRP * lat, ch), 1)

    def fields(i0, shift):
        wind = wind_v[pl.ds(i0, GRP)].reshape(GRP * lat, ch).astype(jnp.float32) * 0.5
        turned = pltpu.roll(wind, half, 1)
        cx = jnp.where(lane2 < half, wind, turned).reshape(shape)
        cy = jnp.where(lane2 < half, turned, wind).reshape(shape)
        near = pltpu.roll(diffusion_ref[...], shift, 1)
        dif = jnp.concatenate([jnp.broadcast_to(near[:, g:g + 1], (lat, ch))[None] for g in range(GRP)], axis=0)
        return cx, cy, dif

    for k in range(PIECES):
        winds[k].wait()

        @pl.loop(k * part // GRP, (k + 1) * part // GRP)
        def _(c):
            i0 = pl.multiple_of(c * GRP, GRP)

            def get(di, dj):
                return tile[pl.ds(i0 + 1 + di, GRP), pl.ds(PAD + dj, lat), :]

            mid, e, w, n, s = get(0, 0), get(1, 0), get(-1, 0), get(0, 1), get(0, -1)
            cx, cy, dif = fields(i0, lax.rem(lon - i0, lon))
            coef_n[pl.ds(i0, GRP)] = (dif - cy)[:, lat - 8:]
            coef_s[pl.ds(i0, GRP)] = (dif + cy)[:, :8]
            laplace = e + w + n + s - 4.0 * mid
            adv_ref[pl.ds(i0, GRP)] = mid - cx * (e - w) - cy * (n - s) + dif * laplace

    cx, _, dif = fields(0, 0)
    coef_w[...] = (dif + cx)[:1]
    cx, _, dif = fields(lon - GRP, GRP)
    coef_e[...] = (dif - cx)[GRP - 1:]

    to_e.wait()
    to_w.wait()
    adv_ref[pl.ds(0, 1)] = adv_ref[pl.ds(0, 1)] + coef_w[...] * halo_w[...]
    adv_ref[pl.ds(lon - 1, 1)] = adv_ref[pl.ds(lon - 1, 1)] + coef_e[...] * halo_e[...]

    @pl.when(has_n)
    def _():
        to_n.wait_send()
        to_s.wait_recv()

    @pl.when(has_s)
    def _():
        to_s.wait_send()
        to_n.wait_recv()

    sub = iota((2 * GRP, 8, ch), 1)

    @pl.loop(0, lon // (2 * GRP))
    def _(c):
        r = pl.ds(pl.multiple_of(c * 2 * GRP, 2 * GRP), 2 * GRP)
        lo, hi = pl.ds(0, 8), pl.ds(lat - 8, 8)
        adv_ref[r, lo, :] = adv_ref[r, lo, :] + jnp.where(sub == 0, coef_s[r] * halo_s[r], 0.0)
        adv_ref[r, hi, :] = adv_ref[r, hi, :] + jnp.where(sub == 7, coef_n[r] * halo_n[r], 0.0)

    for cp in weights:
        cp.wait()


def silu(v):
    hv = 0.5 * v
    return (hv + hv * jnp.tanh(hv)).astype(jnp.bfloat16)


def closure_kernel(adv, place, turned, base_v, win, whid0, whid_hbm, wout_hbm, out_hbm,
                   done, packed, ha, hb, whid, wout, base_s, bsem, wsem, osem):
    cols, ch = done.shape
    chunks = cols // CHUNK
    per = CHUNK // adv.shape[1]
    layers = whid.shape[0] + 1
    cp_base = pltpu.make_async_copy(base_v, base_s, bsem)
    cp_base.start()
    weights = [pltpu.make_async_copy(whid_hbm.at[pl.ds(l + 1, 1)], whid.at[pl.ds(l, 1)], wsem.at[l])
               for l in range(layers - 1)]
    weights.append(pltpu.make_async_copy(wout_hbm, wout, wsem.at[layers - 1]))
    for cp in weights:
        cp.start()
    packed[...] = jnp.zeros_like(packed)
    cp_base.wait()

    sub = iota((CHUNK, CHUNK), 0).astype(jnp.float32)
    lane = iota((CHUNK, CHUNK), 1).astype(jnp.float32)

    for c in range(chunks):
        pick = onezero(sub == place[pl.ds(c, 1), :])
        feats = adv[pl.ds(c * per, per)].reshape(CHUNK, ch).astype(jnp.bfloat16)
        packed[pl.ds(base_s[c, 0], CHUNK), :] = mm(pick, feats)

    for cp in weights:
        cp.wait()
    hid = win.shape[1]

    @pl.loop(0, cols // 2 // TM)
    def _(t):
        r = pl.ds(pl.multiple_of(t * TM, TM), TM)
        x = packed[r, :].astype(jnp.bfloat16)
        for n in range(0, hid, STEP):
            ha[:, n:n + STEP] = silu(mm(x, win[:, n:n + STEP]))
        src, dst = ha, hb
        for l in range(layers):
            w, i = (whid0, 0) if l == 0 else (whid, l - 1)
            for n in range(0, hid, STEP):
                dst[:, n:n + STEP] = silu(mm(src[...], w[i, :, n:n + STEP]))
            src, dst = dst, src
        packed[r, :] = mm(src[...], wout[...])

    outs = []
    group = 2
    for c in range(chunks):
        tend = packed[pl.ds(base_s[c, 0], CHUNK), :].astype(jnp.bfloat16)
        back = onezero(lane == turned[:, c:c + 1])
        done[pl.ds(c * CHUNK, CHUNK), :] = adv[pl.ds(c * per, per)].reshape(CHUNK, ch) + mm(back, tend)
        if c % group == group - 1:
            r = pl.ds((c + 1 - group) * CHUNK, group * CHUNK)
            cp = pltpu.make_async_copy(done.at[r, :], out_hbm.at[r, :], osem.at[c // group])
            cp.start()
            outs.append(cp)
    for cp in outs:
        cp.wait()


def local(ntx, nty, state, courant, diffusion, conv_mask, w_in, w_hidden, w_out):
    lon, lat, ch = state.shape
    cols = lon * lat
    hid = w_in.shape[1]
    layers = w_hidden.shape[0]
    chunks = cols // CHUNK
    vmem = pl.BlockSpec(memory_space=pltpu.VMEM)
    hbm = pl.BlockSpec(memory_space=pltpu.MemorySpace.HBM)
    adv, win, whid0, place, turned, base = pl.pallas_call(
        functools.partial(advance_kernel, ntx, nty),
        out_shape=[
            pltpu.VMEM((lon, lat, ch), jnp.float32),
            pltpu.VMEM(w_in.shape, jnp.bfloat16),
            pltpu.VMEM((1, hid, hid), jnp.bfloat16),
            pltpu.VMEM((chunks, CHUNK), jnp.float32),
            pltpu.VMEM((CHUNK, chunks), jnp.float32),
            pltpu.VMEM((chunks, CHUNK), jnp.int32),
        ],
        in_specs=[hbm, hbm, vmem, vmem, hbm, hbm],
        out_specs=[vmem] * 6,
        scratch_shapes=[
            pltpu.VMEM((lon + 2, lat + 2 * PAD, ch), jnp.float32),
            pltpu.VMEM((lon, lat, ch), jnp.bfloat16),
            pltpu.VMEM((lon, 1, ch), jnp.float32),
            pltpu.VMEM((lon, 1, ch), jnp.float32),
            pltpu.VMEM((lon, 1, ch), jnp.float32),
            pltpu.VMEM((lon, 1, ch), jnp.float32),
            pltpu.VMEM((1, lat, ch), jnp.float32),
            pltpu.VMEM((1, lat, ch), jnp.float32),
            pltpu.VMEM((lon, 8, ch), jnp.float32),
            pltpu.VMEM((lon, 8, ch), jnp.float32),
            pltpu.VMEM((1, lat, ch), jnp.float32),
            pltpu.VMEM((1, lat, ch), jnp.float32),
            pltpu.SemaphoreType.DMA((PIECES,)),
            pltpu.SemaphoreType.DMA((PIECES,)),
            pltpu.SemaphoreType.DMA((2,)),
            pltpu.SemaphoreType.DMA((4,)),
            pltpu.SemaphoreType.DMA((4,)),
        ],
        compiler_params=pltpu.CompilerParams(collective_id=0, has_side_effects=True,
                                             vmem_limit_bytes=ROOM),
        name="advance",
    )(state, courant, diffusion.T, conv_mask.T, w_in, w_hidden)
    out = pl.pallas_call(
        closure_kernel,
        out_shape=jax.ShapeDtypeStruct((cols, ch), jnp.float32),
        in_specs=[vmem] * 6 + [hbm] * 2,
        out_specs=hbm,
        scratch_shapes=[
            pltpu.VMEM((cols, ch), jnp.float32),
            pltpu.VMEM((cols // 2 + CHUNK, ch), jnp.float32),
            pltpu.VMEM((TM, hid), jnp.bfloat16),
            pltpu.VMEM((TM, hid), jnp.bfloat16),
            pltpu.VMEM((layers - 1, hid, hid), jnp.bfloat16),
            pltpu.VMEM(w_out.shape, jnp.bfloat16),
            pltpu.SMEM((chunks, CHUNK), jnp.int32),
            pltpu.SemaphoreType.DMA,
            pltpu.SemaphoreType.DMA((layers,)),
            pltpu.SemaphoreType.DMA((chunks,)),
        ],
        compiler_params=pltpu.CompilerParams(vmem_limit_bytes=ROOM // 2),
        name="closure",
    )(adv, place, turned, base, win, whid0, w_hidden, w_out)
    return out.reshape(lon, lat, ch)


def solution(mesh):
    spec = P(("member", "tx"), "ty", None)
    flat = P(("member", "tx"), "ty")
    return jax.shard_map(
        functools.partial(local, mesh.shape["tx"], mesh.shape["ty"]),
        mesh=mesh,
        in_specs=(spec, spec, flat, flat, P(), P(), P()),
        out_specs=spec,
        check_vma=False,
    )
```

```python
import functools

import jax
import jax.numpy as jnp
from jax import lax
from jax.experimental import pallas as pl
from jax.experimental.pallas import tpu as pltpu
from jax.sharding import PartitionSpec as P

MESH = pl.DeviceIdType.MESH
PAD = 8
PIECES = 4
CHUNK = 128
EDGES = 8
STEP = 256
GRANTS = (53 << 20, 41 << 20, 24 << 20)


def onezero(cond):
    return cond.astype(jnp.float32).astype(jnp.bfloat16)


def iota(shape, dim):
    return lax.broadcasted_iota(jnp.int32, shape, dim)


def mm(a, b, dims=((1,), (0,))):
    return lax.dot_general(a, b, (dims, ((), ())), preferred_element_type=jnp.float32)


def silu(v):
    hv = 0.5 * v
    return (hv + hv * jnp.tanh(hv)).astype(jnp.bfloat16)


def mlp(load, store, win, first, later, wout, ha, hb, hooks):
    hid = win.shape[1]
    x = load()
    src, dst = None, ha
    for l in range(later.shape[0] + 2):
        if l in hooks:
            hooks[l]()
        for n in range(0, hid, STEP):
            cut = slice(n, n + STEP)
            w = win[:, cut] if l == 0 else first[0, :, cut] if l == 1 else later[l - 2, :, cut]
            dst[:, cut] = silu(mm(x if l == 0 else src[...], w))
        src, dst = dst, (hb if dst is ha else ha)
    store(mm(src[...], wout[...]))


def prepare_kernel(state_hbm, courant_hbm, diffusion_hbm, mask_hbm, whid_hbm,
                   adv_ref, packed, edge_n, edge_s, edge_e, edge_w, coef_n, coef_s, coef_e, coef_w,
                   first_ref, place_ref, turned_ref, base_ref,
                   tile, wind_v, dif_v, diffusion_ref, mask_ref, base_s, lsem, csem, wsem, bsem):
    lon, lat, ch = wind_v.shape
    part = lon // PIECES
    per = CHUNK // lat
    chunks = lon // per
    tm = lon * lat // 4

    loads = [pltpu.make_async_copy(state_hbm.at[pl.ds(k * part, part)],
                                   tile.at[pl.ds(1 + k * part, part), pl.ds(PAD, lat)], lsem.at[k])
             for k in range(PIECES)]
    winds = [pltpu.make_async_copy(courant_hbm.at[pl.ds(k * part, part)],
                                   wind_v.at[pl.ds(k * part, part)], csem.at[k])
             for k in range(PIECES)]
    weight = pltpu.make_async_copy(whid_hbm.at[pl.ds(0, 1)], first_ref, wsem.at[0])
    small = [pltpu.make_async_copy(mask_hbm, mask_ref, wsem.at[1]),
             pltpu.make_async_copy(diffusion_hbm, diffusion_ref, wsem.at[2])]
    for cp in small:
        cp.start()
    for k in range(PIECES):
        loads[k].start()
        winds[k].start()
    weight.start()

    edge = jnp.zeros((lon, 1, ch), jnp.float32)
    tile[pl.ds(1, lon), pl.ds(PAD - 1, 1), :] = edge
    tile[pl.ds(1, lon), pl.ds(PAD + lat, 1), :] = edge
    tile[pl.ds(0, 1), pl.ds(PAD, lat), :] = jnp.zeros((1, lat, ch), jnp.float32)
    tile[pl.ds(lon + 1, 1), pl.ds(PAD, lat), :] = jnp.zeros((1, lat, ch), jnp.float32)
    packed[...] = jnp.zeros_like(packed)
    for cp in small:
        cp.wait()

    flags = mask_ref[...].astype(jnp.float32)
    spread = onezero(iota((lat, CHUNK), 1) % lat == iota((lat, CHUNK), 0))
    rep = mm(flags.astype(jnp.bfloat16), spread, ((0,), (0,)))
    keep = iota((lon, CHUNK), 1) // lat == iota((lon, CHUNK), 0) % per
    rep = jnp.where(keep, rep, 0.0).astype(jnp.bfloat16)
    fold = onezero(iota((chunks, lon), 1) // per == iota((chunks, lon), 0))
    rows = mm(fold, rep)
    row, col = iota((chunks, CHUNK), 0), iota((chunks, CHUNK), 1)
    rim = (col % lat == 0) | (col % lat == lat - 1)
    ends = ((row == 0) & (col < lat)) | ((row == chunks - 1) & (col >= CHUNK - lat))
    ew = jnp.sum(jnp.where(ends & jnp.logical_not(rim), rows, 0.0), axis=0, keepdims=True)
    edges = jnp.concatenate([flags[:1], flags[lat - 1:], ew, jnp.zeros((EDGES - 3, CHUNK), jnp.float32)], axis=0)
    rows = jnp.concatenate([jnp.where(rim | ends, 0.0, rows), edges], axis=0)
    rows_b = rows.astype(jnp.bfloat16)
    first, second = iota((CHUNK, CHUNK), 0), iota((CHUNK, CHUNK), 1)
    rank = mm(rows_b, onezero(first < second))
    rank_t = mm(onezero(second < first), rows_b, ((1,), (1,)))
    rows_t = mm(onezero(first == second), rows_b, ((1,), (1,)))
    place_ref[...] = jnp.where(rows > 0.5, rank, -1.0)
    turned_ref[...] = jnp.where(rows_t > 0.5, rank_t, -1.0)
    total = jnp.broadcast_to(jnp.sum(rows, axis=1, keepdims=True), rows.shape)
    both = (chunks + EDGES,) * 2
    base = mm(onezero(iota(both, 1) < iota(both, 0)), total.astype(jnp.bfloat16))
    shift = jnp.maximum(tm - base[chunks:chunks + 1], 0.0)
    base = base + jnp.where(iota(base.shape, 0) >= chunks, shift, 0.0)
    base_ref[...] = base.astype(jnp.int32)
    cp_base = pltpu.make_async_copy(base_ref, base_s, bsem)
    cp_base.start()

    for i in range(lon):
        dif_v[i] = jnp.broadcast_to(diffusion_ref[:, i:i + 1], (lat, ch))

    half = ch // 2
    lane = iota((lat, ch), 1)

    def fields(i):
        wind = wind_v[i].astype(jnp.float32)
        turned = pltpu.roll(wind, half, 1)
        cx = jnp.where(lane < half, wind, turned)
        cy = jnp.where(lane < half, turned, wind)
        return cx, cy, dif_v[i]

    sub = iota((CHUNK, CHUNK), 0).astype(jnp.float32)

    def pack(k):
        for c in range(k * part // per, (k + 1) * part // per):
            pick = onezero(sub == place_ref[pl.ds(c, 1), :])
            feats = adv_ref[pl.ds(c * per, per)].reshape(CHUNK, ch).astype(jnp.bfloat16)
            packed[pl.ds(base_s[c, 0], CHUNK), :] = mm(pick, feats)

    for k in range(PIECES):
        winds[k].wait()
        for piece in ([0, 1] if k == 0 else [k + 1]):
            if piece < PIECES:
                loads[piece].wait()
        if k == 1:
            cp_base.wait()
        for i in range(k * part, (k + 1) * part):

            def get(di, dj):
                return tile[i + 1 + di, pl.ds(PAD + dj, lat), :]

            mid, e, w, n, s = get(0, 0), get(1, 0), get(-1, 0), get(0, 1), get(0, -1)
            cx, cy, dif = fields(i)
            coef_n[i] = (dif - 0.5 * cy)[lat - 8:]
            coef_s[i] = (dif + 0.5 * cy)[:8]
            laplace = (e + w) + (n + s) - 4.0 * mid
            adv_ref[i] = mid - 0.5 * (cx * (e - w) + cy * (n - s)) + dif * laplace
        if k > 0:
            pack(k - 1)

    cx, _, dif = fields(0)
    coef_w[...] = dif + 0.5 * cx
    cx, _, dif = fields(lon - 1)
    coef_e[...] = dif - 0.5 * cx
    pitch = lat + 2 * PAD
    flat = tile.reshape((lon + 2) * pitch, ch)
    edge_n[...] = flat[pl.ds(pitch + PAD + lat - 1, lon, stride=pitch), :]
    edge_s[...] = flat[pl.ds(pitch + PAD, lon, stride=pitch), :]
    edge_e[...] = tile[lon, pl.ds(PAD, lat), :]
    edge_w[...] = tile[1, pl.ds(PAD, lat), :]
    pack(PIECES - 1)
    weight.wait()


def first_kernel(ntx, nty, packed, edge_n, edge_s, edge_e, edge_w, win, first, wout, whid_hbm,
                 tend, later, got_n, got_s, got_e, got_w,
                 ha, hb, wsem, ssem, rsem):
    ix, iy = lax.axis_index("tx"), lax.axis_index("ty")
    east, west = lax.rem(ix + 1, ntx), lax.rem(ix + ntx - 1, ntx)
    has_n, has_s = iy < nty - 1, iy > 0
    tm = ha.shape[0]

    barrier = pltpu.get_barrier_semaphore()
    pl.semaphore_signal(barrier, inc=1, device_id={"tx": east}, device_id_type=MESH)
    pl.semaphore_signal(barrier, inc=1, device_id={"tx": west}, device_id_type=MESH)

    @pl.when(has_n)
    def _():
        pl.semaphore_signal(barrier, inc=1, device_id={"ty": iy + 1}, device_id_type=MESH)

    @pl.when(has_s)
    def _():
        pl.semaphore_signal(barrier, inc=1, device_id={"ty": iy - 1}, device_id_type=MESH)

    weights = [pltpu.make_async_copy(whid_hbm.at[pl.ds(l + 1, 1)], later.at[pl.ds(l, 1)], wsem.at[l])
               for l in range(later.shape[0])]
    for cp in weights:
        cp.start()

    @pl.when(jnp.logical_not(has_n))
    def _():
        got_n[...] = jnp.zeros_like(got_n)

    @pl.when(jnp.logical_not(has_s))
    def _():
        got_s[...] = jnp.zeros_like(got_s)

    def send(src, dst, k, dev):
        return pltpu.make_async_remote_copy(
            src_ref=src, dst_ref=dst, send_sem=ssem.at[k], recv_sem=rsem.at[k],
            device_id=dev, device_id_type=MESH)

    to_n = send(edge_n, got_s, 2, {"ty": iy + 1})
    to_s = send(edge_s, got_n, 3, {"ty": iy - 1})
    to_e = send(edge_e, got_w, 0, {"tx": east})
    to_w = send(edge_w, got_e, 1, {"tx": west})

    def meet():
        pl.semaphore_wait(barrier, 2 + has_n.astype(jnp.int32) + has_s.astype(jnp.int32))
        pl.when(has_n)(to_n.start)
        pl.when(has_s)(to_s.start)
        to_e.start()
        to_w.start()

    def pause():
        for cp in weights:
            cp.wait()
        meet()

    hooks = {2: pause}

    def store(value):
        tend[...] = value

    mlp(lambda: packed[pl.ds(0, tm), :].astype(jnp.bfloat16), store, win, first, later, wout, ha, hb, hooks)

    to_e.wait()
    to_w.wait()

    @pl.when(has_n)
    def _():
        to_n.wait_send()
        to_s.wait_recv()

    @pl.when(has_s)
    def _():
        to_s.wait_send()
        to_n.wait_recv()


def second_kernel(adv, packed, head, halo_n, halo_s, halo_e, halo_w, coef_n, coef_s, coef_e, coef_w,
                  place, turned, base_v, win, first, later, wout, out_hbm,
                  done, work, tend, rim_s, rim_n, rim_ew, ha, hb, base_s, bsem, osem):
    lon, lat, ch = adv.shape
    cols = lon * lat
    chunks = cols // CHUNK
    per = CHUNK // lat
    tm = ha.shape[0]
    cp_base = pltpu.make_async_copy(base_v, base_s, bsem)
    cp_base.start()

    flat = adv.reshape(cols, ch)
    south, north = coef_s.reshape(lon * 8, ch), coef_n.reshape(lon * 8, ch)
    rim_s[...] = flat[pl.ds(0, lon, stride=lat), :] + south[pl.ds(0, lon, stride=8), :] * halo_s[...]
    rim_n[...] = flat[pl.ds(lat - 1, lon, stride=lat), :] + north[pl.ds(7, lon, stride=8), :] * halo_n[...]
    add_w, add_e = coef_w[...] * halo_w[...], coef_e[...] * halo_e[...]
    rim_s[pl.ds(0, 1), :] = rim_s[pl.ds(0, 1), :] + add_w[:1]
    rim_n[pl.ds(0, 1), :] = rim_n[pl.ds(0, 1), :] + add_w[lat - 1:]
    rim_s[pl.ds(lon - 1, 1), :] = rim_s[pl.ds(lon - 1, 1), :] + add_e[:1]
    rim_n[pl.ds(lon - 1, 1), :] = rim_n[pl.ds(lon - 1, 1), :] + add_e[lat - 1:]
    rim_ew[...] = jnp.zeros_like(rim_ew)
    rim_ew[pl.ds(0, lat), :] = adv[0] + add_w
    rim_ew[pl.ds(CHUNK - lat, lat), :] = adv[lon - 1] + add_e

    work[...] = packed[pl.ds(tm, tm + CHUNK), :]
    tend[pl.ds(0, tm), :] = head[...]
    tend[pl.ds(2 * tm, CHUNK), :] = jnp.zeros((CHUNK, ch), jnp.float32)
    cp_base.wait()

    sub = iota((CHUNK, CHUNK), 0).astype(jnp.float32)
    lane = iota((CHUNK, CHUNK), 1).astype(jnp.float32)
    rims = (rim_s, rim_n, rim_ew)
    for k, rim in enumerate(rims):
        pick = onezero(sub == place[pl.ds(chunks + k, 1), :])
        work[pl.ds(base_s[chunks + k, 0] - tm, CHUNK), :] = mm(pick, rim[...].astype(jnp.bfloat16))

    def store(value):
        tend[pl.ds(tm, tm), :] = value

    mlp(lambda: work[pl.ds(0, tm), :].astype(jnp.bfloat16), store, win, first, later, wout, ha, hb, {})

    def spread(c):
        rows = tend[pl.ds(base_s[c, 0], CHUNK), :].astype(jnp.bfloat16)
        return mm(onezero(lane == turned[:, c:c + 1]), rows)

    for k, rim in enumerate(rims):
        rim[...] = rim[...] + spread(chunks + k)

    outs = []
    group = 2
    for c in range(chunks):
        done[pl.ds(c * CHUNK, CHUNK), :] = flat[pl.ds(c * CHUNK, CHUNK), :] + spread(c)
        if c == 0:
            done[pl.ds(0, lat), :] = rim_ew[pl.ds(0, lat), :]
        if c == chunks - 1:
            done[pl.ds(cols - lat, lat), :] = rim_ew[pl.ds(CHUNK - lat, lat), :]
        for i in range(c * per, (c + 1) * per):
            done[pl.ds(i * lat, 1), :] = rim_s[pl.ds(i, 1), :]
            done[pl.ds(i * lat + lat - 1, 1), :] = rim_n[pl.ds(i, 1), :]
        if c % group == group - 1:
            r = pl.ds((c + 1 - group) * CHUNK, group * CHUNK)
            cp = pltpu.make_async_copy(done.at[r, :], out_hbm.at[r, :], osem.at[c // group])
            cp.start()
            outs.append(cp)
    for cp in outs:
        cp.wait()


def local(ntx, nty, state, courant, diffusion, conv_mask, w_in, w_hidden, w_out):
    lon, lat, ch = state.shape
    assert lon == CHUNK
    cols = lon * lat
    hid = w_in.shape[1]
    layers = w_hidden.shape[0]
    chunks = cols // CHUNK
    tm = cols // 4
    f32, bf16 = jnp.float32, jnp.bfloat16
    vmem = pl.BlockSpec(memory_space=pltpu.VMEM)
    hbm = pl.BlockSpec(memory_space=pltpu.MemorySpace.HBM)
    (adv, packed, edge_n, edge_s, edge_e, edge_w, coef_n, coef_s, coef_e, coef_w,
     first, place, turned, base) = pl.pallas_call(
        prepare_kernel,
        out_shape=[
            pltpu.VMEM((lon, lat, ch), f32),
            pltpu.VMEM((2 * tm + CHUNK, ch), f32),
            pltpu.VMEM((lon, ch), f32),
            pltpu.VMEM((lon, ch), f32),
            pltpu.VMEM((lat, ch), f32),
            pltpu.VMEM((lat, ch), f32),
            pltpu.VMEM((lon, 8, ch), f32),
            pltpu.VMEM((lon, 8, ch), f32),
            pltpu.VMEM((lat, ch), f32),
            pltpu.VMEM((lat, ch), f32),
            pltpu.VMEM((1, hid, hid), bf16),
            pltpu.VMEM((chunks + EDGES, CHUNK), f32),
            pltpu.VMEM((CHUNK, chunks + EDGES), f32),
            pltpu.VMEM((chunks + EDGES, CHUNK), jnp.int32),
        ],
        in_specs=[hbm] * 5,
        out_specs=[vmem] * 14,
        scratch_shapes=[
            pltpu.VMEM((lon + 2, lat + 2 * PAD, ch), f32),
            pltpu.VMEM((lon, lat, ch), bf16),
            pltpu.VMEM((lon, lat, ch), f32),
            pltpu.VMEM((lat, lon), f32),
            pltpu.VMEM((lat, lon), jnp.int32),
            pltpu.SMEM((chunks + EDGES, CHUNK), jnp.int32),
            pltpu.SemaphoreType.DMA((PIECES,)),
            pltpu.SemaphoreType.DMA((PIECES,)),
            pltpu.SemaphoreType.DMA((3,)),
            pltpu.SemaphoreType.DMA,
        ],
        compiler_params=pltpu.CompilerParams(vmem_limit_bytes=GRANTS[0]),
        name="prepare",
    )(state, courant, diffusion.T, conv_mask.T, w_hidden)
    head, later, halo_n, halo_s, halo_e, halo_w = pl.pallas_call(
        functools.partial(first_kernel, ntx, nty),
        out_shape=[
            pltpu.VMEM((tm, ch), f32),
            pltpu.VMEM((layers - 1, hid, hid), bf16),
            pltpu.VMEM((lon, ch), f32),
            pltpu.VMEM((lon, ch), f32),
            pltpu.VMEM((lat, ch), f32),
            pltpu.VMEM((lat, ch), f32),
        ],
        in_specs=[vmem] * 8 + [hbm],
        out_specs=[vmem] * 6,
        scratch_shapes=[
            pltpu.VMEM((tm, hid), bf16),
            pltpu.VMEM((tm, hid), bf16),
            pltpu.SemaphoreType.DMA((layers - 1,)),
            pltpu.SemaphoreType.DMA((4,)),
            pltpu.SemaphoreType.DMA((4,)),
        ],
        compiler_params=pltpu.CompilerParams(collective_id=0, has_side_effects=True,
                                             vmem_limit_bytes=GRANTS[1]),
        name="first",
    )(packed, edge_n, edge_s, edge_e, edge_w, w_in, first, w_out, w_hidden)
    out = pl.pallas_call(
        second_kernel,
        out_shape=jax.ShapeDtypeStruct((cols, ch), f32),
        in_specs=[vmem] * 18,
        out_specs=hbm,
        scratch_shapes=[
            pltpu.VMEM((cols, ch), f32),
            pltpu.VMEM((tm + CHUNK, ch), f32),
            pltpu.VMEM((2 * tm + CHUNK, ch), f32),
            pltpu.VMEM((lon, ch), f32),
            pltpu.VMEM((lon, ch), f32),
            pltpu.VMEM((CHUNK, ch), f32),
            pltpu.VMEM((tm, hid), bf16),
            pltpu.VMEM((tm, hid), bf16),
            pltpu.SMEM((chunks + EDGES, CHUNK), jnp.int32),
            pltpu.SemaphoreType.DMA,
            pltpu.SemaphoreType.DMA((chunks,)),
        ],
        compiler_params=pltpu.CompilerParams(vmem_limit_bytes=GRANTS[2]),
        name="second",
    )(adv, packed, head, halo_n, halo_s, halo_e, halo_w, coef_n, coef_s, coef_e, coef_w,
      place, turned, base, w_in, first, later, w_out)
    return out.reshape(lon, lat, ch)


def solution(mesh):
    spec = P(("member", "tx"), "ty", None)
    flat = P(("member", "tx"), "ty")
    return jax.shard_map(
        functools.partial(local, mesh.shape["tx"], mesh.shape["ty"]),
        mesh=mesh,
        in_specs=(spec, spec, flat, flat, P(), P(), P()),
        out_specs=spec,
        check_vma=False,
    )
```

```python
import functools

import jax
import jax.numpy as jnp
from jax import lax
from jax.experimental import pallas as pl
from jax.experimental.pallas import tpu as pltpu
from jax.sharding import PartitionSpec as P

MESH = pl.DeviceIdType.MESH
PAD = 8
PIECES = 4
CHUNK = 128
EDGES = 8
STEP = 256
GRANTS = (50 << 20, 24 << 20, 24 << 20)


def onezero(cond):
    return cond.astype(jnp.float32).astype(jnp.bfloat16)


def iota(shape, dim):
    return lax.broadcasted_iota(jnp.int32, shape, dim)


def mm(a, b, dims=((1,), (0,))):
    return lax.dot_general(a, b, (dims, ((), ())), preferred_element_type=jnp.float32)


def silu(v):
    hv = 0.5 * v
    return (hv + hv * jnp.tanh(hv)).astype(jnp.bfloat16)


def mlp(load, store, win, whid, wout, ha, hb):
    hid = win.shape[1]
    x = load()
    src, dst = None, ha
    for l in range(whid.shape[0] + 1):
        for n in range(0, hid, STEP):
            cut = slice(n, n + STEP)
            w = win[:, cut] if l == 0 else whid[l - 1, :, cut]
            dst[:, cut] = silu(mm(x if l == 0 else src[...], w))
        src, dst = dst, (hb if dst is ha else ha)
    store(mm(src[...], wout[...]))


def prepare_kernel(state_hbm, courant_hbm, diffusion_hbm, mask_hbm, whid_hbm,
                   adv_ref, packed, edge_n, edge_s, edge_e, edge_w, coef_n, coef_s, coef_e, coef_w,
                   whid_ref, place_ref, turned_ref, base_ref,
                   tile, wind_v, dif_v, diffusion_ref, mask_ref, base_s, lsem, csem, wsem, bsem):
    lon, lat, ch = wind_v.shape
    part = lon // PIECES
    per = CHUNK // lat
    chunks = lon // per
    tm = lon * lat // 4

    loads = [pltpu.make_async_copy(state_hbm.at[pl.ds(k * part, part)],
                                   tile.at[pl.ds(1 + k * part, part), pl.ds(PAD, lat)], lsem.at[k])
             for k in range(PIECES)]
    winds = [pltpu.make_async_copy(courant_hbm.at[pl.ds(k * part, part)],
                                   wind_v.at[pl.ds(k * part, part)], csem.at[k])
             for k in range(PIECES)]
    weight = pltpu.make_async_copy(whid_hbm, whid_ref, wsem.at[0])
    small = [pltpu.make_async_copy(mask_hbm, mask_ref, wsem.at[1]),
             pltpu.make_async_copy(diffusion_hbm, diffusion_ref, wsem.at[2])]
    for cp in small:
        cp.start()
    for k in range(PIECES):
        loads[k].start()
        winds[k].start()
    weight.start()

    edge = jnp.zeros((lon, 1, ch), jnp.float32)
    tile[pl.ds(1, lon), pl.ds(PAD - 1, 1), :] = edge
    tile[pl.ds(1, lon), pl.ds(PAD + lat, 1), :] = edge
    tile[pl.ds(0, 1), pl.ds(PAD, lat), :] = jnp.zeros((1, lat, ch), jnp.float32)
    tile[pl.ds(lon + 1, 1), pl.ds(PAD, lat), :] = jnp.zeros((1, lat, ch), jnp.float32)
    packed[...] = jnp.zeros_like(packed)
    for cp in small:
        cp.wait()

    flags = mask_ref[...].astype(jnp.float32)
    spread = onezero(iota((lat, CHUNK), 1) % lat == iota((lat, CHUNK), 0))
    rep = mm(flags.astype(jnp.bfloat16), spread, ((0,), (0,)))
    keep = iota((lon, CHUNK), 1) // lat == iota((lon, CHUNK), 0) % per
    rep = jnp.where(keep, rep, 0.0).astype(jnp.bfloat16)
    fold = onezero(iota((chunks, lon), 1) // per == iota((chunks, lon), 0))
    rows = mm(fold, rep)
    row, col = iota((chunks, CHUNK), 0), iota((chunks, CHUNK), 1)
    rim = (col % lat == 0) | (col % lat == lat - 1)
    ends = ((row == 0) & (col < lat)) | ((row == chunks - 1) & (col >= CHUNK - lat))
    ew = jnp.sum(jnp.where(ends & jnp.logical_not(rim), rows, 0.0), axis=0, keepdims=True)
    edges = jnp.concatenate([flags[:1], flags[lat - 1:], ew, jnp.zeros((EDGES - 3, CHUNK), jnp.float32)], axis=0)
    rows = jnp.concatenate([jnp.where(rim | ends, 0.0, rows), edges], axis=0)
    rows_b = rows.astype(jnp.bfloat16)
    first, second = iota((CHUNK, CHUNK), 0), iota((CHUNK, CHUNK), 1)
    rank = mm(rows_b, onezero(first < second))
    rank_t = mm(onezero(second < first), rows_b, ((1,), (1,)))
    rows_t = mm(onezero(first == second), rows_b, ((1,), (1,)))
    place_ref[...] = jnp.where(rows > 0.5, rank, -1.0)
    turned_ref[...] = jnp.where(rows_t > 0.5, rank_t, -1.0)
    total = jnp.broadcast_to(jnp.sum(rows, axis=1, keepdims=True), rows.shape)
    both = (chunks + EDGES,) * 2
    base = mm(onezero(iota(both, 1) < iota(both, 0)), total.astype(jnp.bfloat16))
    shift = jnp.maximum(tm - base[chunks:chunks + 1], 0.0)
    base = base + jnp.where(iota(base.shape, 0) >= chunks, shift, 0.0)
    base_ref[...] = base.astype(jnp.int32)
    cp_base = pltpu.make_async_copy(base_ref, base_s, bsem)
    cp_base.start()

    for i in range(lon):
        dif_v[i] = jnp.broadcast_to(diffusion_ref[:, i:i + 1], (lat, ch))

    half = ch // 2
    lane = iota((lat, ch), 1)

    def fields(i):
        wind = wind_v[i].astype(jnp.float32)
        turned = pltpu.roll(wind, half, 1)
        cx = jnp.where(lane < half, wind, turned)
        cy = jnp.where(lane < half, turned, wind)
        return cx, cy, dif_v[i]

    sub = iota((CHUNK, CHUNK), 0).astype(jnp.float32)

    def pack(k):
        for c in range(k * part // per, (k + 1) * part // per):
            pick = onezero(sub == place_ref[pl.ds(c, 1), :])
            feats = adv_ref[pl.ds(c * per, per)].reshape(CHUNK, ch).astype(jnp.bfloat16)
            packed[pl.ds(base_s[c, 0], CHUNK), :] = mm(pick, feats)

    for k in range(PIECES):
        winds[k].wait()
        for piece in ([0, 1] if k == 0 else [k + 1]):
            if piece < PIECES:
                loads[piece].wait()
        if k == 1:
            cp_base.wait()
        for i in range(k * part, (k + 1) * part):

            def get(di, dj):
                return tile[i + 1 + di, pl.ds(PAD + dj, lat), :]

            mid, e, w, n, s = get(0, 0), get(1, 0), get(-1, 0), get(0, 1), get(0, -1)
            cx, cy, dif = fields(i)
            coef_n[i] = (dif - 0.5 * cy)[lat - 8:]
            coef_s[i] = (dif + 0.5 * cy)[:8]
            laplace = (e + w) + (n + s) - 4.0 * mid
            adv_ref[i] = mid - 0.5 * (cx * (e - w) + cy * (n - s)) + dif * laplace
        if k > 0:
            pack(k - 1)

    cx, _, dif = fields(0)
    coef_w[...] = dif + 0.5 * cx
    cx, _, dif = fields(lon - 1)
    coef_e[...] = dif - 0.5 * cx
    pitch = lat + 2 * PAD
    flat = tile.reshape((lon + 2) * pitch, ch)
    edge_n[...] = flat[pl.ds(pitch + PAD + lat - 1, lon, stride=pitch), :]
    edge_s[...] = flat[pl.ds(pitch + PAD, lon, stride=pitch), :]
    edge_e[...] = tile[lon, pl.ds(PAD, lat), :]
    edge_w[...] = tile[1, pl.ds(PAD, lat), :]
    pack(PIECES - 1)
    weight.wait()


def first_kernel(ntx, nty, packed, edge_n, edge_s, edge_e, edge_w, win, whid, wout,
                 tend, got_n, got_s, got_e, got_w,
                 ha, hb, ssem, rsem):
    ix, iy = lax.axis_index("tx"), lax.axis_index("ty")
    east, west = lax.rem(ix + 1, ntx), lax.rem(ix + ntx - 1, ntx)
    has_n, has_s = iy < nty - 1, iy > 0
    tm = ha.shape[0]

    barrier = pltpu.get_barrier_semaphore()
    pl.semaphore_signal(barrier, inc=1, device_id={"tx": east}, device_id_type=MESH)
    pl.semaphore_signal(barrier, inc=1, device_id={"tx": west}, device_id_type=MESH)

    @pl.when(has_n)
    def _():
        pl.semaphore_signal(barrier, inc=1, device_id={"ty": iy + 1}, device_id_type=MESH)

    @pl.when(has_s)
    def _():
        pl.semaphore_signal(barrier, inc=1, device_id={"ty": iy - 1}, device_id_type=MESH)

    @pl.when(jnp.logical_not(has_n))
    def _():
        got_n[...] = jnp.zeros_like(got_n)

    @pl.when(jnp.logical_not(has_s))
    def _():
        got_s[...] = jnp.zeros_like(got_s)

    def send(src, dst, k, dev):
        return pltpu.make_async_remote_copy(
            src_ref=src, dst_ref=dst, send_sem=ssem.at[k], recv_sem=rsem.at[k],
            device_id=dev, device_id_type=MESH)

    to_n = send(edge_n, got_s, 2, {"ty": iy + 1})
    to_s = send(edge_s, got_n, 3, {"ty": iy - 1})
    to_e = send(edge_e, got_w, 0, {"tx": east})
    to_w = send(edge_w, got_e, 1, {"tx": west})

    def meet():
        pl.semaphore_wait(barrier, 2 + has_n.astype(jnp.int32) + has_s.astype(jnp.int32))
        pl.when(has_n)(to_n.start)
        pl.when(has_s)(to_s.start)
        to_e.start()
        to_w.start()

    def tile(at, size):
        r = pl.ds(at, size)

        def store(value):
            tend[r, :] = value

        mlp(lambda: packed[r, :].astype(jnp.bfloat16), store, win, whid, wout, ha.at[r], hb.at[r])

    tile(0, tm // 4)
    meet()
    tile(tm // 4, tm - tm // 4)

    to_e.wait()
    to_w.wait()

    @pl.when(has_n)
    def _():
        to_n.wait_send()
        to_s.wait_recv()

    @pl.when(has_s)
    def _():
        to_s.wait_send()
        to_n.wait_recv()


def second_kernel(adv, packed, head, halo_n, halo_s, halo_e, halo_w, coef_n, coef_s, coef_e, coef_w,
                  place, turned, base_v, win, whid, wout, out_hbm,
                  done, work, tend, rim_s, rim_n, rim_ew, ha, hb, base_s, bsem, osem):
    lon, lat, ch = adv.shape
    cols = lon * lat
    chunks = cols // CHUNK
    per = CHUNK // lat
    tm = ha.shape[0]
    cp_base = pltpu.make_async_copy(base_v, base_s, bsem)
    cp_base.start()

    flat = adv.reshape(cols, ch)
    south, north = coef_s.reshape(lon * 8, ch), coef_n.reshape(lon * 8, ch)
    rim_s[...] = flat[pl.ds(0, lon, stride=lat), :] + south[pl.ds(0, lon, stride=8), :] * halo_s[...]
    rim_n[...] = flat[pl.ds(lat - 1, lon, stride=lat), :] + north[pl.ds(7, lon, stride=8), :] * halo_n[...]
    add_w, add_e = coef_w[...] * halo_w[...], coef_e[...] * halo_e[...]
    rim_s[pl.ds(0, 1), :] = rim_s[pl.ds(0, 1), :] + add_w[:1]
    rim_n[pl.ds(0, 1), :] = rim_n[pl.ds(0, 1), :] + add_w[lat - 1:]
    rim_s[pl.ds(lon - 1, 1), :] = rim_s[pl.ds(lon - 1, 1), :] + add_e[:1]
    rim_n[pl.ds(lon - 1, 1), :] = rim_n[pl.ds(lon - 1, 1), :] + add_e[lat - 1:]
    rim_ew[...] = jnp.zeros_like(rim_ew)
    rim_ew[pl.ds(0, lat), :] = adv[0] + add_w
    rim_ew[pl.ds(CHUNK - lat, lat), :] = adv[lon - 1] + add_e

    work[...] = packed[pl.ds(tm, tm + CHUNK), :]
    tend[pl.ds(0, tm), :] = head[...]
    tend[pl.ds(2 * tm, CHUNK), :] = jnp.zeros((CHUNK, ch), jnp.float32)
    cp_base.wait()

    sub = iota((CHUNK, CHUNK), 0).astype(jnp.float32)
    lane = iota((CHUNK, CHUNK), 1).astype(jnp.float32)
    rims = (rim_s, rim_n, rim_ew)
    for k, rim in enumerate(rims):
        pick = onezero(sub == place[pl.ds(chunks + k, 1), :])
        work[pl.ds(base_s[chunks + k, 0] - tm, CHUNK), :] = mm(pick, rim[...].astype(jnp.bfloat16))

    def store(value):
        tend[pl.ds(tm, tm), :] = value

    mlp(lambda: work[pl.ds(0, tm), :].astype(jnp.bfloat16), store, win, whid, wout, ha, hb)

    def spread(c):
        rows = tend[pl.ds(base_s[c, 0], CHUNK), :].astype(jnp.bfloat16)
        return mm(onezero(lane == turned[:, c:c + 1]), rows)

    for k, rim in enumerate(rims):
        rim[...] = rim[...] + spread(chunks + k)

    outs = []
    group = 2
    for c in range(chunks):
        done[pl.ds(c * CHUNK, CHUNK), :] = flat[pl.ds(c * CHUNK, CHUNK), :] + spread(c)
        if c == 0:
            done[pl.ds(0, lat), :] = rim_ew[pl.ds(0, lat), :]
        if c == chunks - 1:
            done[pl.ds(cols - lat, lat), :] = rim_ew[pl.ds(CHUNK - lat, lat), :]
        for i in range(c * per, (c + 1) * per):
            done[pl.ds(i * lat, 1), :] = rim_s[pl.ds(i, 1), :]
            done[pl.ds(i * lat + lat - 1, 1), :] = rim_n[pl.ds(i, 1), :]
        if c % group == group - 1:
            r = pl.ds((c + 1 - group) * CHUNK, group * CHUNK)
            cp = pltpu.make_async_copy(done.at[r, :], out_hbm.at[r, :], osem.at[c // group])
            cp.start()
            outs.append(cp)
    for cp in outs:
        cp.wait()


def local(ntx, nty, state, courant, diffusion, conv_mask, w_in, w_hidden, w_out):
    lon, lat, ch = state.shape
    assert lon == CHUNK
    cols = lon * lat
    hid = w_in.shape[1]
    chunks = cols // CHUNK
    tm = cols // 4
    f32, bf16 = jnp.float32, jnp.bfloat16
    vmem = pl.BlockSpec(memory_space=pltpu.VMEM)
    hbm = pl.BlockSpec(memory_space=pltpu.MemorySpace.HBM)
    (adv, packed, edge_n, edge_s, edge_e, edge_w, coef_n, coef_s, coef_e, coef_w,
     whid, place, turned, base) = pl.pallas_call(
        prepare_kernel,
        out_shape=[
            pltpu.VMEM((lon, lat, ch), f32),
            pltpu.VMEM((2 * tm + CHUNK, ch), f32),
            pltpu.VMEM((lon, ch), f32),
            pltpu.VMEM((lon, ch), f32),
            pltpu.VMEM((lat, ch), f32),
            pltpu.VMEM((lat, ch), f32),
            pltpu.VMEM((lon, 8, ch), f32),
            pltpu.VMEM((lon, 8, ch), f32),
            pltpu.VMEM((lat, ch), f32),
            pltpu.VMEM((lat, ch), f32),
            pltpu.VMEM(w_hidden.shape, bf16),
            pltpu.VMEM((chunks + EDGES, CHUNK), f32),
            pltpu.VMEM((CHUNK, chunks + EDGES), f32),
            pltpu.VMEM((chunks + EDGES, CHUNK), jnp.int32),
        ],
        in_specs=[hbm] * 5,
        out_specs=[vmem] * 14,
        scratch_shapes=[
            pltpu.VMEM((lon + 2, lat + 2 * PAD, ch), f32),
            pltpu.VMEM((lon, lat, ch), bf16),
            pltpu.VMEM((lon, lat, ch), f32),
            pltpu.VMEM((lat, lon), f32),
            pltpu.VMEM((lat, lon), jnp.int32),
            pltpu.SMEM((chunks + EDGES, CHUNK), jnp.int32),
            pltpu.SemaphoreType.DMA((PIECES,)),
            pltpu.SemaphoreType.DMA((PIECES,)),
            pltpu.SemaphoreType.DMA((3,)),
            pltpu.SemaphoreType.DMA,
        ],
        compiler_params=pltpu.CompilerParams(vmem_limit_bytes=GRANTS[0]),
        name="prepare",
    )(state, courant, diffusion.T, conv_mask.T, w_hidden)
    head, halo_n, halo_s, halo_e, halo_w = pl.pallas_call(
        functools.partial(first_kernel, ntx, nty),
        out_shape=[
            pltpu.VMEM((tm, ch), f32),
            pltpu.VMEM((lon, ch), f32),
            pltpu.VMEM((lon, ch), f32),
            pltpu.VMEM((lat, ch), f32),
            pltpu.VMEM((lat, ch), f32),
        ],
        in_specs=[vmem] * 8,
        out_specs=[vmem] * 5,
        scratch_shapes=[
            pltpu.VMEM((tm, hid), bf16),
            pltpu.VMEM((tm, hid), bf16),
            pltpu.SemaphoreType.DMA((4,)),
            pltpu.SemaphoreType.DMA((4,)),
        ],
        compiler_params=pltpu.CompilerParams(collective_id=0, has_side_effects=True,
                                             vmem_limit_bytes=GRANTS[1]),
        name="first",
    )(packed, edge_n, edge_s, edge_e, edge_w, w_in, whid, w_out)
    out = pl.pallas_call(
        second_kernel,
        out_shape=jax.ShapeDtypeStruct((cols, ch), f32),
        in_specs=[vmem] * 17,
        out_specs=hbm,
        scratch_shapes=[
            pltpu.VMEM((cols, ch), f32),
            pltpu.VMEM((tm + CHUNK, ch), f32),
            pltpu.VMEM((2 * tm + CHUNK, ch), f32),
            pltpu.VMEM((lon, ch), f32),
            pltpu.VMEM((lon, ch), f32),
            pltpu.VMEM((CHUNK, ch), f32),
            pltpu.VMEM((tm, hid), bf16),
            pltpu.VMEM((tm, hid), bf16),
            pltpu.SMEM((chunks + EDGES, CHUNK), jnp.int32),
            pltpu.SemaphoreType.DMA,
            pltpu.SemaphoreType.DMA((chunks,)),
        ],
        compiler_params=pltpu.CompilerParams(vmem_limit_bytes=GRANTS[2]),
        name="second",
    )(adv, packed, head, halo_n, halo_s, halo_e, halo_w, coef_n, coef_s, coef_e, coef_w,
      place, turned, base, w_in, whid, w_out)
    return out.reshape(lon, lat, ch)


def solution(mesh):
    spec = P(("member", "tx"), "ty", None)
    flat = P(("member", "tx"), "ty")
    return jax.shard_map(
        functools.partial(local, mesh.shape["tx"], mesh.shape["ty"]),
        mesh=mesh,
        in_specs=(spec, spec, flat, flat, P(), P(), P()),
        out_specs=spec,
        check_vma=False,
    )
```

```python
import functools

import jax
import jax.numpy as jnp
from jax import lax
from jax.experimental import pallas as pl
from jax.experimental.pallas import tpu as pltpu
from jax.sharding import PartitionSpec as P

MESH = pl.DeviceIdType.MESH
PAD = 8
PIECES = 4
CHUNK = 128
EDGES = 8
STEP = 256
GRANTS = (50 << 20, 24 << 20, 24 << 20)


def onezero(cond):
    return cond.astype(jnp.float32).astype(jnp.bfloat16)


def iota(shape, dim):
    return lax.broadcasted_iota(jnp.int32, shape, dim)


def mm(a, b, dims=((1,), (0,))):
    return lax.dot_general(a, b, (dims, ((), ())), preferred_element_type=jnp.float32)


def silu(v):
    hv = 0.5 * v
    return (hv + hv * jnp.tanh(hv)).astype(jnp.bfloat16)


def mlp(load, store, win, whid, wout, ha, hb):
    hid = win.shape[1]
    x = load()
    src, dst = None, ha
    for l in range(whid.shape[0] + 1):
        for n in range(0, hid, STEP):
            cut = slice(n, n + STEP)
            w = win[:, cut] if l == 0 else whid[l - 1, :, cut]
            dst[:, cut] = silu(mm(x if l == 0 else src[...], w))
        src, dst = dst, (hb if dst is ha else ha)
    store(mm(src[...], wout[...]))


def prepare_kernel(state_hbm, courant_hbm, diffusion_hbm, mask_hbm, whid_hbm,
                   adv_ref, packed, edge_n, edge_s, edge_e, edge_w, coef_n, coef_s, coef_e, coef_w,
                   whid_ref, place_ref, turned_ref, base_ref,
                   tile, wind_v, dif_v, diffusion_ref, mask_ref, base_s, lsem, csem, wsem, bsem):
    lon, lat, ch = wind_v.shape
    part = lon // PIECES
    per = CHUNK // lat
    chunks = lon // per
    tm = lon * lat // 4

    loads = [pltpu.make_async_copy(state_hbm.at[pl.ds(k * part, part)],
                                   tile.at[pl.ds(1 + k * part, part), pl.ds(PAD, lat)], lsem.at[k])
             for k in range(PIECES)]
    winds = [pltpu.make_async_copy(courant_hbm.at[pl.ds(k * part, part)],
                                   wind_v.at[pl.ds(k * part, part)], csem.at[k])
             for k in range(PIECES)]
    weight = pltpu.make_async_copy(whid_hbm, whid_ref, wsem.at[0])
    small = [pltpu.make_async_copy(mask_hbm, mask_ref, wsem.at[1]),
             pltpu.make_async_copy(diffusion_hbm, diffusion_ref, wsem.at[2])]
    for cp in small:
        cp.start()
    for k in range(PIECES):
        loads[k].start()
        winds[k].start()
    weight.start()

    edge = jnp.zeros((lon, 1, ch), jnp.float32)
    tile[pl.ds(1, lon), pl.ds(PAD - 1, 1), :] = edge
    tile[pl.ds(1, lon), pl.ds(PAD + lat, 1), :] = edge
    tile[pl.ds(0, 1), pl.ds(PAD, lat), :] = jnp.zeros((1, lat, ch), jnp.float32)
    tile[pl.ds(lon + 1, 1), pl.ds(PAD, lat), :] = jnp.zeros((1, lat, ch), jnp.float32)
    packed[...] = jnp.zeros_like(packed)
    for cp in small:
        cp.wait()

    flags = mask_ref[...].astype(jnp.float32)
    spread = onezero(iota((lat, CHUNK), 1) % lat == iota((lat, CHUNK), 0))
    rep = mm(flags.astype(jnp.bfloat16), spread, ((0,), (0,)))
    keep = iota((lon, CHUNK), 1) // lat == iota((lon, CHUNK), 0) % per
    rep = jnp.where(keep, rep, 0.0).astype(jnp.bfloat16)
    fold = onezero(iota((chunks, lon), 1) // per == iota((chunks, lon), 0))
    rows = mm(fold, rep)
    row, col = iota((chunks, CHUNK), 0), iota((chunks, CHUNK), 1)
    rim = (col % lat == 0) | (col % lat == lat - 1)
    ends = ((row == 0) & (col < lat)) | ((row == chunks - 1) & (col >= CHUNK - lat))
    ew = jnp.sum(jnp.where(ends & jnp.logical_not(rim), rows, 0.0), axis=0, keepdims=True)
    edges = jnp.concatenate([flags[:1], flags[lat - 1:], ew, jnp.zeros((EDGES - 3, CHUNK), jnp.float32)], axis=0)
    rows = jnp.concatenate([jnp.where(rim | ends, 0.0, rows), edges], axis=0)
    rows_b = rows.astype(jnp.bfloat16)
    first, second = iota((CHUNK, CHUNK), 0), iota((CHUNK, CHUNK), 1)
    rank = mm(rows_b, onezero(first < second))
    rank_t = mm(onezero(second < first), rows_b, ((1,), (1,)))
    rows_t = mm(onezero(first == second), rows_b, ((1,), (1,)))
    place_ref[...] = jnp.where(rows > 0.5, rank, -1.0)
    turned_ref[...] = jnp.where(rows_t > 0.5, rank_t, -1.0)
    total = jnp.broadcast_to(jnp.sum(rows, axis=1, keepdims=True), rows.shape)
    both = (chunks + EDGES,) * 2
    base = mm(onezero(iota(both, 1) < iota(both, 0)), total.astype(jnp.bfloat16))
    shift = jnp.maximum(tm - base[chunks:chunks + 1], 0.0)
    base = base + jnp.where(iota(base.shape, 0) >= chunks, shift, 0.0)
    base_ref[...] = base.astype(jnp.int32)
    cp_base = pltpu.make_async_copy(base_ref, base_s, bsem)
    cp_base.start()

    for i in range(lon):
        dif_v[i] = jnp.broadcast_to(diffusion_ref[:, i:i + 1], (lat, ch))

    half = ch // 2
    lane = iota((lat, ch), 1)

    def fields(i):
        wind = wind_v[i].astype(jnp.float32)
        turned = pltpu.roll(wind, half, 1)
        cx = jnp.where(lane < half, wind, turned)
        cy = jnp.where(lane < half, turned, wind)
        return cx, cy, dif_v[i]

    sub = iota((CHUNK, CHUNK), 0).astype(jnp.float32)

    def pack(k):
        for c in range(k * part // per, (k + 1) * part // per):
            pick = onezero(sub == place_ref[pl.ds(c, 1), :])
            feats = adv_ref[pl.ds(c * per, per)].reshape(CHUNK, ch).astype(jnp.bfloat16)
            packed[pl.ds(base_s[c, 0], CHUNK), :] = mm(pick, feats)

    for k in range(PIECES):
        winds[k].wait()
        for piece in ([0, 1] if k == 0 else [k + 1]):
            if piece < PIECES:
                loads[piece].wait()
        if k == PIECES - 1:
            cp_base.wait()
        for i in range(k * part, (k + 1) * part):

            def get(di, dj):
                return tile[i + 1 + di, pl.ds(PAD + dj, lat), :]

            mid, e, w, n, s = get(0, 0), get(1, 0), get(-1, 0), get(0, 1), get(0, -1)
            cx, cy, dif = fields(i)
            coef_n[i] = (dif - 0.5 * cy)[lat - 8:]
            coef_s[i] = (dif + 0.5 * cy)[:8]
            laplace = (e + w) + (n + s) - 4.0 * mid
            adv_ref[i] = mid - 0.5 * (cx * (e - w) + cy * (n - s)) + dif * laplace
        if k == PIECES - 1:
            for early in range(k):
                pack(early)

    cx, _, dif = fields(0)
    coef_w[...] = dif + 0.5 * cx
    cx, _, dif = fields(lon - 1)
    coef_e[...] = dif - 0.5 * cx
    pitch = lat + 2 * PAD
    flat = tile.reshape((lon + 2) * pitch, ch)
    edge_n[...] = flat[pl.ds(pitch + PAD + lat - 1, lon, stride=pitch), :]
    edge_s[...] = flat[pl.ds(pitch + PAD, lon, stride=pitch), :]
    edge_e[...] = tile[lon, pl.ds(PAD, lat), :]
    edge_w[...] = tile[1, pl.ds(PAD, lat), :]
    pack(PIECES - 1)
    weight.wait()


def first_kernel(ntx, nty, packed, edge_n, edge_s, edge_e, edge_w, win, whid, wout,
                 tend, got_n, got_s, got_e, got_w,
                 ha, hb, ssem, rsem):
    ix, iy = lax.axis_index("tx"), lax.axis_index("ty")
    east, west = lax.rem(ix + 1, ntx), lax.rem(ix + ntx - 1, ntx)
    has_n, has_s = iy < nty - 1, iy > 0
    tm = ha.shape[0]

    barrier = pltpu.get_barrier_semaphore()
    pl.semaphore_signal(barrier, inc=1, device_id={"tx": east}, device_id_type=MESH)
    pl.semaphore_signal(barrier, inc=1, device_id={"tx": west}, device_id_type=MESH)

    @pl.when(has_n)
    def _():
        pl.semaphore_signal(barrier, inc=1, device_id={"ty": iy + 1}, device_id_type=MESH)

    @pl.when(has_s)
    def _():
        pl.semaphore_signal(barrier, inc=1, device_id={"ty": iy - 1}, device_id_type=MESH)

    @pl.when(jnp.logical_not(has_n))
    def _():
        got_n[...] = jnp.zeros_like(got_n)

    @pl.when(jnp.logical_not(has_s))
    def _():
        got_s[...] = jnp.zeros_like(got_s)

    def send(src, dst, k, dev):
        return pltpu.make_async_remote_copy(
            src_ref=src, dst_ref=dst, send_sem=ssem.at[k], recv_sem=rsem.at[k],
            device_id=dev, device_id_type=MESH)

    to_n = send(edge_n, got_s, 2, {"ty": iy + 1})
    to_s = send(edge_s, got_n, 3, {"ty": iy - 1})
    to_e = send(edge_e, got_w, 0, {"tx": east})
    to_w = send(edge_w, got_e, 1, {"tx": west})

    def meet():
        pl.semaphore_wait(barrier, 2 + has_n.astype(jnp.int32) + has_s.astype(jnp.int32))
        pl.when(has_n)(to_n.start)
        pl.when(has_s)(to_s.start)
        to_e.start()
        to_w.start()

    def tile(at, size):
        r = pl.ds(at, size)

        def store(value):
            tend[r, :] = value

        mlp(lambda: packed[r, :].astype(jnp.bfloat16), store, win, whid, wout, ha.at[r], hb.at[r])

    tile(0, tm // 4)
    meet()
    tile(tm // 4, tm - tm // 4)

    to_e.wait()
    to_w.wait()

    @pl.when(has_n)
    def _():
        to_n.wait_send()
        to_s.wait_recv()

    @pl.when(has_s)
    def _():
        to_s.wait_send()
        to_n.wait_recv()


def second_kernel(adv, packed, head, halo_n, halo_s, halo_e, halo_w, coef_n, coef_s, coef_e, coef_w,
                  place, turned, base_v, win, whid, wout, out_hbm,
                  done, work, tend, rim_s, rim_n, rim_ew, ha, hb, base_s, bsem, osem):
    lon, lat, ch = adv.shape
    cols = lon * lat
    chunks = cols // CHUNK
    per = CHUNK // lat
    tm = ha.shape[0]
    cp_base = pltpu.make_async_copy(base_v, base_s, bsem)
    cp_base.start()

    flat = adv.reshape(cols, ch)
    south, north = coef_s.reshape(lon * 8, ch), coef_n.reshape(lon * 8, ch)
    rim_s[...] = flat[pl.ds(0, lon, stride=lat), :] + south[pl.ds(0, lon, stride=8), :] * halo_s[...]
    rim_n[...] = flat[pl.ds(lat - 1, lon, stride=lat), :] + north[pl.ds(7, lon, stride=8), :] * halo_n[...]
    add_w, add_e = coef_w[...] * halo_w[...], coef_e[...] * halo_e[...]
    rim_s[pl.ds(0, 1), :] = rim_s[pl.ds(0, 1), :] + add_w[:1]
    rim_n[pl.ds(0, 1), :] = rim_n[pl.ds(0, 1), :] + add_w[lat - 1:]
    rim_s[pl.ds(lon - 1, 1), :] = rim_s[pl.ds(lon - 1, 1), :] + add_e[:1]
    rim_n[pl.ds(lon - 1, 1), :] = rim_n[pl.ds(lon - 1, 1), :] + add_e[lat - 1:]
    rim_ew[...] = jnp.zeros_like(rim_ew)
    rim_ew[pl.ds(0, lat), :] = adv[0] + add_w
    rim_ew[pl.ds(CHUNK - lat, lat), :] = adv[lon - 1] + add_e

    work[...] = packed[pl.ds(tm, tm + CHUNK), :]
    tend[pl.ds(0, tm), :] = head[...]
    tend[pl.ds(2 * tm, CHUNK), :] = jnp.zeros((CHUNK, ch), jnp.float32)

    sub = iota((CHUNK, CHUNK), 0).astype(jnp.float32)
    lane = iota((CHUNK, CHUNK), 1).astype(jnp.float32)
    rims = (rim_s, rim_n, rim_ew)
    for k, rim in enumerate(rims):
        pick = onezero(sub == place[pl.ds(chunks + k, 1), :])
        at = jnp.max(base_v[pl.ds(chunks + k, 1), :].astype(jnp.float32)).astype(jnp.int32)
        work[pl.ds(at - tm, CHUNK), :] = mm(pick, rim[...].astype(jnp.bfloat16))

    def store(value):
        tend[pl.ds(tm, tm), :] = value

    mlp(lambda: work[pl.ds(0, tm), :].astype(jnp.bfloat16), store, win, whid, wout, ha, hb)

    cp_base.wait()

    def spread(c):
        rows = tend[pl.ds(base_s[c, 0], CHUNK), :].astype(jnp.bfloat16)
        return mm(onezero(lane == turned[:, c:c + 1]), rows)

    for k, rim in enumerate(rims):
        rim[...] = rim[...] + spread(chunks + k)

    outs = []
    group = 2
    for c in range(chunks):
        done[pl.ds(c * CHUNK, CHUNK), :] = flat[pl.ds(c * CHUNK, CHUNK), :] + spread(c)
        if c == 0:
            done[pl.ds(0, lat), :] = rim_ew[pl.ds(0, lat), :]
        if c == chunks - 1:
            done[pl.ds(cols - lat, lat), :] = rim_ew[pl.ds(CHUNK - lat, lat), :]
        for i in range(c * per, (c + 1) * per):
            done[pl.ds(i * lat, 1), :] = rim_s[pl.ds(i, 1), :]
            done[pl.ds(i * lat + lat - 1, 1), :] = rim_n[pl.ds(i, 1), :]
        if c % group == group - 1:
            r = pl.ds((c + 1 - group) * CHUNK, group * CHUNK)
            cp = pltpu.make_async_copy(done.at[r, :], out_hbm.at[r, :], osem.at[c // group])
            cp.start()
            outs.append(cp)
    for cp in outs:
        cp.wait()


def local(ntx, nty, state, courant, diffusion, conv_mask, w_in, w_hidden, w_out):
    lon, lat, ch = state.shape
    assert lon == CHUNK
    cols = lon * lat
    hid = w_in.shape[1]
    chunks = cols // CHUNK
    tm = cols // 4
    f32, bf16 = jnp.float32, jnp.bfloat16
    vmem = pl.BlockSpec(memory_space=pltpu.VMEM)
    hbm = pl.BlockSpec(memory_space=pltpu.MemorySpace.HBM)
    (adv, packed, edge_n, edge_s, edge_e, edge_w, coef_n, coef_s, coef_e, coef_w,
     whid, place, turned, base) = pl.pallas_call(
        prepare_kernel,
        out_shape=[
            pltpu.VMEM((lon, lat, ch), f32),
            pltpu.VMEM((2 * tm + CHUNK, ch), f32),
            pltpu.VMEM((lon, ch), f32),
            pltpu.VMEM((lon, ch), f32),
            pltpu.VMEM((lat, ch), f32),
            pltpu.VMEM((lat, ch), f32),
            pltpu.VMEM((lon, 8, ch), f32),
            pltpu.VMEM((lon, 8, ch), f32),
            pltpu.VMEM((lat, ch), f32),
            pltpu.VMEM((lat, ch), f32),
            pltpu.VMEM(w_hidden.shape, bf16),
            pltpu.VMEM((chunks + EDGES, CHUNK), f32),
            pltpu.VMEM((CHUNK, chunks + EDGES), f32),
            pltpu.VMEM((chunks + EDGES, CHUNK), jnp.int32),
        ],
        in_specs=[hbm] * 5,
        out_specs=[vmem] * 14,
        scratch_shapes=[
            pltpu.VMEM((lon + 2, lat + 2 * PAD, ch), f32),
            pltpu.VMEM((lon, lat, ch), bf16),
            pltpu.VMEM((lon, lat, ch), f32),
            pltpu.VMEM((lat, lon), f32),
            pltpu.VMEM((lat, lon), jnp.int32),
            pltpu.SMEM((chunks + EDGES, CHUNK), jnp.int32),
            pltpu.SemaphoreType.DMA((PIECES,)),
            pltpu.SemaphoreType.DMA((PIECES,)),
            pltpu.SemaphoreType.DMA((3,)),
            pltpu.SemaphoreType.DMA,
        ],
        compiler_params=pltpu.CompilerParams(vmem_limit_bytes=GRANTS[0]),
        name="prepare",
    )(state, courant, diffusion.T, conv_mask.T, w_hidden)
    head, halo_n, halo_s, halo_e, halo_w = pl.pallas_call(
        functools.partial(first_kernel, ntx, nty),
        out_shape=[
            pltpu.VMEM((tm, ch), f32),
            pltpu.VMEM((lon, ch), f32),
            pltpu.VMEM((lon, ch), f32),
            pltpu.VMEM((lat, ch), f32),
            pltpu.VMEM((lat, ch), f32),
        ],
        in_specs=[vmem] * 8,
        out_specs=[vmem] * 5,
        scratch_shapes=[
            pltpu.VMEM((tm, hid), bf16),
            pltpu.VMEM((tm, hid), bf16),
            pltpu.SemaphoreType.DMA((4,)),
            pltpu.SemaphoreType.DMA((4,)),
        ],
        compiler_params=pltpu.CompilerParams(collective_id=0, has_side_effects=True,
                                             vmem_limit_bytes=GRANTS[1]),
        name="first",
    )(packed, edge_n, edge_s, edge_e, edge_w, w_in, whid, w_out)
    out = pl.pallas_call(
        second_kernel,
        out_shape=jax.ShapeDtypeStruct((cols, ch), f32),
        in_specs=[vmem] * 17,
        out_specs=hbm,
        scratch_shapes=[
            pltpu.VMEM((cols, ch), f32),
            pltpu.VMEM((tm + CHUNK, ch), f32),
            pltpu.VMEM((2 * tm + CHUNK, ch), f32),
            pltpu.VMEM((lon, ch), f32),
            pltpu.VMEM((lon, ch), f32),
            pltpu.VMEM((CHUNK, ch), f32),
            pltpu.VMEM((tm, hid), bf16),
            pltpu.VMEM((tm, hid), bf16),
            pltpu.SMEM((chunks + EDGES, CHUNK), jnp.int32),
            pltpu.SemaphoreType.DMA,
            pltpu.SemaphoreType.DMA((chunks,)),
        ],
        compiler_params=pltpu.CompilerParams(vmem_limit_bytes=GRANTS[2]),
        name="second",
    )(adv, packed, head, halo_n, halo_s, halo_e, halo_w, coef_n, coef_s, coef_e, coef_w,
      place, turned, base, w_in, whid, w_out)
    return out.reshape(lon, lat, ch)


def solution(mesh):
    spec = P(("member", "tx"), "ty", None)
    flat = P(("member", "tx"), "ty")
    return jax.shard_map(
        functools.partial(local, mesh.shape["tx"], mesh.shape["ty"]),
        mesh=mesh,
        in_specs=(spec, spec, flat, flat, P(), P(), P()),
        out_specs=spec,
        check_vma=False,
    )
```

```python
import functools

import jax
import jax.numpy as jnp
from jax import lax
from jax.experimental import pallas as pl
from jax.experimental.pallas import tpu as pltpu
from jax.sharding import PartitionSpec as P

MESH = pl.DeviceIdType.MESH
PAD = 8
PIECES = 4
CHUNK = 128
EDGES = 8
STEP = 256
GRANTS = (50 << 20, 24 << 20, 24 << 20)


def onezero(cond):
    return cond.astype(jnp.float32).astype(jnp.bfloat16)


def iota(shape, dim):
    return lax.broadcasted_iota(jnp.int32, shape, dim)


def mm(a, b, dims=((1,), (0,))):
    return lax.dot_general(a, b, (dims, ((), ())), preferred_element_type=jnp.float32)


def silu(v):
    hv = 0.5 * v
    return (hv + hv * jnp.tanh(hv)).astype(jnp.bfloat16)


def mlp(load, store, win, whid, wout, ha, hb):
    hid = win.shape[1]
    x = load()
    src, dst = None, ha
    for l in range(whid.shape[0] + 1):
        for n in range(0, hid, STEP):
            cut = slice(n, n + STEP)
            w = win[:, cut] if l == 0 else whid[l - 1, :, cut]
            dst[:, cut] = silu(mm(x if l == 0 else src[...], w))
        src, dst = dst, (hb if dst is ha else ha)
    store(mm(src[...], wout[...]))


def prepare_kernel(state_hbm, courant_hbm, diffusion_hbm, mask_hbm, whid_hbm,
                   adv_ref, packed, edge_n, edge_s, edge_e, edge_w, coef_n, coef_s, coef_e, coef_w,
                   whid_ref, place_ref, turned_ref, base_ref,
                   tile, wind_v, dif_v, diffusion_ref, mask_ref, base_s, lsem, csem, wsem, bsem):
    lon, lat, ch = wind_v.shape
    part = lon // PIECES
    per = CHUNK // lat
    chunks = lon // per
    tm = lon * lat // 4

    loads = [pltpu.make_async_copy(state_hbm.at[pl.ds(k * part, part)],
                                   tile.at[pl.ds(1 + k * part, part), pl.ds(PAD, lat)], lsem.at[k])
             for k in range(PIECES)]
    winds = [pltpu.make_async_copy(courant_hbm.at[pl.ds(k * part, part)],
                                   wind_v.at[pl.ds(k * part, part)], csem.at[k])
             for k in range(PIECES)]
    weight = pltpu.make_async_copy(whid_hbm, whid_ref, wsem.at[0])
    small = [pltpu.make_async_copy(mask_hbm, mask_ref, wsem.at[1]),
             pltpu.make_async_copy(diffusion_hbm, diffusion_ref, wsem.at[2])]
    for cp in small:
        cp.start()
    for k in range(PIECES):
        loads[k].start()
        winds[k].start()
    weight.start()

    edge = jnp.zeros((lon, 1, ch), jnp.float32)
    tile[pl.ds(1, lon), pl.ds(PAD - 1, 1), :] = edge
    tile[pl.ds(1, lon), pl.ds(PAD + lat, 1), :] = edge
    tile[pl.ds(0, 1), pl.ds(PAD, lat), :] = jnp.zeros((1, lat, ch), jnp.float32)
    tile[pl.ds(lon + 1, 1), pl.ds(PAD, lat), :] = jnp.zeros((1, lat, ch), jnp.float32)
    packed[...] = jnp.zeros_like(packed)
    for cp in small:
        cp.wait()

    flags = mask_ref[...].astype(jnp.float32)
    spread = onezero(iota((lat, CHUNK), 1) % lat == iota((lat, CHUNK), 0))
    rep = mm(flags.astype(jnp.bfloat16), spread, ((0,), (0,)))
    keep = iota((lon, CHUNK), 1) // lat == iota((lon, CHUNK), 0) % per
    rep = jnp.where(keep, rep, 0.0).astype(jnp.bfloat16)
    fold = onezero(iota((chunks, lon), 1) // per == iota((chunks, lon), 0))
    rows = mm(fold, rep)
    row, col = iota((chunks, CHUNK), 0), iota((chunks, CHUNK), 1)
    rim = (col % lat == 0) | (col % lat == lat - 1)
    ends = ((row == 0) & (col < lat)) | ((row == chunks - 1) & (col >= CHUNK - lat))
    ew = jnp.sum(jnp.where(ends & jnp.logical_not(rim), rows, 0.0), axis=0, keepdims=True)
    edges = jnp.concatenate([flags[:1], flags[lat - 1:], ew, jnp.zeros((EDGES - 3, CHUNK), jnp.float32)], axis=0)
    rows = jnp.concatenate([jnp.where(rim | ends, 0.0, rows), edges], axis=0)
    rows_b = rows.astype(jnp.bfloat16)
    first, second = iota((CHUNK, CHUNK), 0), iota((CHUNK, CHUNK), 1)
    rank = mm(rows_b, onezero(first < second))
    rank_t = mm(onezero(second < first), rows_b, ((1,), (1,)))
    rows_t = mm(onezero(first == second), rows_b, ((1,), (1,)))
    place_ref[...] = jnp.where(rows > 0.5, rank, -1.0)
    turned_ref[...] = jnp.where(rows_t > 0.5, rank_t, -1.0)
    total = jnp.broadcast_to(jnp.sum(rows, axis=1, keepdims=True), rows.shape)
    both = (chunks + EDGES,) * 2
    base = mm(onezero(iota(both, 1) < iota(both, 0)), total.astype(jnp.bfloat16))
    shift = jnp.maximum(tm - base[chunks:chunks + 1], 0.0)
    base = base + jnp.where(iota(base.shape, 0) >= chunks, shift, 0.0)
    base_ref[...] = base.astype(jnp.int32)
    cp_base = pltpu.make_async_copy(base_ref, base_s, bsem)
    cp_base.start()

    for i in range(lon):
        dif_v[i] = jnp.broadcast_to(diffusion_ref[:, i:i + 1], (lat, ch))

    half = ch // 2
    lane = iota((lat, ch), 1)

    def fields(i):
        wind = wind_v[i].astype(jnp.float32)
        turned = pltpu.roll(wind, half, 1)
        cx = jnp.where(lane < half, wind, turned)
        cy = jnp.where(lane < half, turned, wind)
        return cx, cy, dif_v[i]

    sub = iota((CHUNK, CHUNK), 0).astype(jnp.float32)

    def pack(k):
        for c in range(k * part // per, (k + 1) * part // per):
            pick = onezero(sub == place_ref[pl.ds(c, 1), :])
            feats = adv_ref[pl.ds(c * per, per)].reshape(CHUNK, ch).astype(jnp.bfloat16)
            packed[pl.ds(base_s[c, 0], CHUNK), :] = mm(pick, feats)

    for k in range(PIECES):
        winds[k].wait()
        for piece in ([0, 1] if k == 0 else [k + 1]):
            if piece < PIECES:
                loads[piece].wait()
        if k == PIECES - 1:
            cp_base.wait()
        for i in range(k * part, (k + 1) * part):

            def get(di, dj):
                return tile[i + 1 + di, pl.ds(PAD + dj, lat), :]

            mid, e, w, n, s = get(0, 0), get(1, 0), get(-1, 0), get(0, 1), get(0, -1)
            cx, cy, dif = fields(i)
            coef_n[i] = (dif - 0.5 * cy)[lat - 8:]
            coef_s[i] = (dif + 0.5 * cy)[:8]
            laplace = (e + w) + (n + s) - 4.0 * mid
            adv_ref[i] = mid - 0.5 * (cx * (e - w) + cy * (n - s)) + dif * laplace
        if k == PIECES - 1:
            for early in range(k):
                pack(early)

    cx, _, dif = fields(0)
    coef_w[...] = dif + 0.5 * cx
    cx, _, dif = fields(lon - 1)
    coef_e[...] = dif - 0.5 * cx
    pitch = lat + 2 * PAD
    flat = tile.reshape((lon + 2) * pitch, ch)
    edge_n[...] = flat[pl.ds(pitch + PAD + lat - 1, lon, stride=pitch), :]
    edge_s[...] = flat[pl.ds(pitch + PAD, lon, stride=pitch), :]
    edge_e[...] = tile[lon, pl.ds(PAD, lat), :]
    edge_w[...] = tile[1, pl.ds(PAD, lat), :]
    pack(PIECES - 1)
    weight.wait()


def first_kernel(ntx, nty, packed, edge_n, edge_s, edge_e, edge_w, win, whid, wout,
                 tend, got_n, got_s, got_e, got_w,
                 ha, hb, ssem, rsem):
    ix, iy = lax.axis_index("tx"), lax.axis_index("ty")
    east, west = lax.rem(ix + 1, ntx), lax.rem(ix + ntx - 1, ntx)
    has_n, has_s = iy < nty - 1, iy > 0
    tm = ha.shape[0]

    barrier = pltpu.get_barrier_semaphore()
    pl.semaphore_signal(barrier, inc=1, device_id={"tx": east}, device_id_type=MESH)
    pl.semaphore_signal(barrier, inc=1, device_id={"tx": west}, device_id_type=MESH)

    @pl.when(has_n)
    def _():
        pl.semaphore_signal(barrier, inc=1, device_id={"ty": iy + 1}, device_id_type=MESH)

    @pl.when(has_s)
    def _():
        pl.semaphore_signal(barrier, inc=1, device_id={"ty": iy - 1}, device_id_type=MESH)

    @pl.when(jnp.logical_not(has_n))
    def _():
        got_n[...] = jnp.zeros_like(got_n)

    @pl.when(jnp.logical_not(has_s))
    def _():
        got_s[...] = jnp.zeros_like(got_s)

    def send(src, dst, k, dev):
        return pltpu.make_async_remote_copy(
            src_ref=src, dst_ref=dst, send_sem=ssem.at[k], recv_sem=rsem.at[k],
            device_id=dev, device_id_type=MESH)

    to_n = send(edge_n, got_s, 2, {"ty": iy + 1})
    to_s = send(edge_s, got_n, 3, {"ty": iy - 1})
    to_e = send(edge_e, got_w, 0, {"tx": east})
    to_w = send(edge_w, got_e, 1, {"tx": west})

    def meet():
        pl.semaphore_wait(barrier, 2 + has_n.astype(jnp.int32) + has_s.astype(jnp.int32))
        pl.when(has_n)(to_n.start)
        pl.when(has_s)(to_s.start)
        to_e.start()
        to_w.start()

    def tile(at, size):
        r = pl.ds(at, size)

        def store(value):
            tend[r, :] = value

        mlp(lambda: packed[r, :].astype(jnp.bfloat16), store, win, whid, wout, ha.at[r], hb.at[r])

    tile(0, tm // 4)
    meet()
    tile(tm // 4, tm - tm // 4)

    to_e.wait()
    to_w.wait()

    @pl.when(has_n)
    def _():
        to_n.wait_send()
        to_s.wait_recv()

    @pl.when(has_s)
    def _():
        to_s.wait_send()
        to_n.wait_recv()


def second_kernel(adv, packed, head, halo_n, halo_s, halo_e, halo_w, coef_n, coef_s, coef_e, coef_w,
                  place, turned, base_v, win, whid, wout, out_hbm,
                  done, work, tend, back, rim_s, rim_n, rim_ew, ha, hb, base_s, bsem, osem):
    lon, lat, ch = adv.shape
    cols = lon * lat
    chunks = cols // CHUNK
    per = CHUNK // lat
    tm = ha.shape[0]
    cp_base = pltpu.make_async_copy(base_v, base_s, bsem)
    cp_base.start()

    flat = adv.reshape(cols, ch)
    south, north = coef_s.reshape(lon * 8, ch), coef_n.reshape(lon * 8, ch)
    rim_s[...] = flat[pl.ds(0, lon, stride=lat), :] + south[pl.ds(0, lon, stride=8), :] * halo_s[...]
    rim_n[...] = flat[pl.ds(lat - 1, lon, stride=lat), :] + north[pl.ds(7, lon, stride=8), :] * halo_n[...]
    add_w, add_e = coef_w[...] * halo_w[...], coef_e[...] * halo_e[...]
    rim_s[pl.ds(0, 1), :] = rim_s[pl.ds(0, 1), :] + add_w[:1]
    rim_n[pl.ds(0, 1), :] = rim_n[pl.ds(0, 1), :] + add_w[lat - 1:]
    rim_s[pl.ds(lon - 1, 1), :] = rim_s[pl.ds(lon - 1, 1), :] + add_e[:1]
    rim_n[pl.ds(lon - 1, 1), :] = rim_n[pl.ds(lon - 1, 1), :] + add_e[lat - 1:]
    rim_ew[...] = jnp.zeros_like(rim_ew)
    rim_ew[pl.ds(0, lat), :] = adv[0] + add_w
    rim_ew[pl.ds(CHUNK - lat, lat), :] = adv[lon - 1] + add_e

    work[...] = packed[pl.ds(tm, tm + CHUNK), :]
    tend[pl.ds(0, tm), :] = head[...]
    tend[pl.ds(2 * tm, CHUNK), :] = jnp.zeros((CHUNK, ch), jnp.float32)

    sub = iota((CHUNK, CHUNK), 0).astype(jnp.float32)
    lane = iota((CHUNK, CHUNK), 1).astype(jnp.float32)
    rims = (rim_s, rim_n, rim_ew)
    for k, rim in enumerate(rims):
        pick = onezero(sub == place[pl.ds(chunks + k, 1), :])
        at = jnp.max(base_v[pl.ds(chunks + k, 1), :].astype(jnp.float32)).astype(jnp.int32)
        work[pl.ds(at - tm, CHUNK), :] = mm(pick, rim[...].astype(jnp.bfloat16))

    for c in range(chunks + len(rims)):
        back[c] = onezero(lane == turned[:, c:c + 1])

    def store(value):
        tend[pl.ds(tm, tm), :] = value

    mlp(lambda: work[pl.ds(0, tm), :].astype(jnp.bfloat16), store, win, whid, wout, ha, hb)

    cp_base.wait()

    def spread(c):
        rows = tend[pl.ds(base_s[c, 0], CHUNK), :].astype(jnp.bfloat16)
        return mm(back[c], rows)

    for k, rim in enumerate(rims):
        rim[...] = rim[...] + spread(chunks + k)

    outs = []
    group = 2
    for c in range(chunks):
        done[pl.ds(c * CHUNK, CHUNK), :] = flat[pl.ds(c * CHUNK, CHUNK), :] + spread(c)
        if c == 0:
            done[pl.ds(0, lat), :] = rim_ew[pl.ds(0, lat), :]
        if c == chunks - 1:
            done[pl.ds(cols - lat, lat), :] = rim_ew[pl.ds(CHUNK - lat, lat), :]
        for i in range(c * per, (c + 1) * per):
            done[pl.ds(i * lat, 1), :] = rim_s[pl.ds(i, 1), :]
            done[pl.ds(i * lat + lat - 1, 1), :] = rim_n[pl.ds(i, 1), :]
        if c % group == group - 1:
            r = pl.ds((c + 1 - group) * CHUNK, group * CHUNK)
            cp = pltpu.make_async_copy(done.at[r, :], out_hbm.at[r, :], osem.at[c // group])
            cp.start()
            outs.append(cp)
    for cp in outs:
        cp.wait()


def local(ntx, nty, state, courant, diffusion, conv_mask, w_in, w_hidden, w_out):
    lon, lat, ch = state.shape
    assert lon == CHUNK
    cols = lon * lat
    hid = w_in.shape[1]
    chunks = cols // CHUNK
    tm = cols // 4
    f32, bf16 = jnp.float32, jnp.bfloat16
    vmem = pl.BlockSpec(memory_space=pltpu.VMEM)
    hbm = pl.BlockSpec(memory_space=pltpu.MemorySpace.HBM)
    (adv, packed, edge_n, edge_s, edge_e, edge_w, coef_n, coef_s, coef_e, coef_w,
     whid, place, turned, base) = pl.pallas_call(
        prepare_kernel,
        out_shape=[
            pltpu.VMEM((lon, lat, ch), f32),
            pltpu.VMEM((2 * tm + CHUNK, ch), f32),
            pltpu.VMEM((lon, ch), f32),
            pltpu.VMEM((lon, ch), f32),
            pltpu.VMEM((lat, ch), f32),
            pltpu.VMEM((lat, ch), f32),
            pltpu.VMEM((lon, 8, ch), f32),
            pltpu.VMEM((lon, 8, ch), f32),
            pltpu.VMEM((lat, ch), f32),
            pltpu.VMEM((lat, ch), f32),
            pltpu.VMEM(w_hidden.shape, bf16),
            pltpu.VMEM((chunks + EDGES, CHUNK), f32),
            pltpu.VMEM((CHUNK, chunks + EDGES), f32),
            pltpu.VMEM((chunks + EDGES, CHUNK), jnp.int32),
        ],
        in_specs=[hbm] * 5,
        out_specs=[vmem] * 14,
        scratch_shapes=[
            pltpu.VMEM((lon + 2, lat + 2 * PAD, ch), f32),
            pltpu.VMEM((lon, lat, ch), bf16),
            pltpu.VMEM((lon, lat, ch), f32),
            pltpu.VMEM((lat, lon), f32),
            pltpu.VMEM((lat, lon), jnp.int32),
            pltpu.SMEM((chunks + EDGES, CHUNK), jnp.int32),
            pltpu.SemaphoreType.DMA((PIECES,)),
            pltpu.SemaphoreType.DMA((PIECES,)),
            pltpu.SemaphoreType.DMA((3,)),
            pltpu.SemaphoreType.DMA,
        ],
        compiler_params=pltpu.CompilerParams(vmem_limit_bytes=GRANTS[0]),
        name="prepare",
    )(state, courant, diffusion.T, conv_mask.T, w_hidden)
    head, halo_n, halo_s, halo_e, halo_w = pl.pallas_call(
        functools.partial(first_kernel, ntx, nty),
        out_shape=[
            pltpu.VMEM((tm, ch), f32),
            pltpu.VMEM((lon, ch), f32),
            pltpu.VMEM((lon, ch), f32),
            pltpu.VMEM((lat, ch), f32),
            pltpu.VMEM((lat, ch), f32),
        ],
        in_specs=[vmem] * 8,
        out_specs=[vmem] * 5,
        scratch_shapes=[
            pltpu.VMEM((tm, hid), bf16),
            pltpu.VMEM((tm, hid), bf16),
            pltpu.SemaphoreType.DMA((4,)),
            pltpu.SemaphoreType.DMA((4,)),
        ],
        compiler_params=pltpu.CompilerParams(collective_id=0, has_side_effects=True,
                                             vmem_limit_bytes=GRANTS[1]),
        name="first",
    )(packed, edge_n, edge_s, edge_e, edge_w, w_in, whid, w_out)
    out = pl.pallas_call(
        second_kernel,
        out_shape=jax.ShapeDtypeStruct((cols, ch), f32),
        in_specs=[vmem] * 17,
        out_specs=hbm,
        scratch_shapes=[
            pltpu.VMEM((cols, ch), f32),
            pltpu.VMEM((tm + CHUNK, ch), f32),
            pltpu.VMEM((2 * tm + CHUNK, ch), f32),
            pltpu.VMEM((chunks + EDGES, CHUNK, CHUNK), bf16),
            pltpu.VMEM((lon, ch), f32),
            pltpu.VMEM((lon, ch), f32),
            pltpu.VMEM((CHUNK, ch), f32),
            pltpu.VMEM((tm, hid), bf16),
            pltpu.VMEM((tm, hid), bf16),
            pltpu.SMEM((chunks + EDGES, CHUNK), jnp.int32),
            pltpu.SemaphoreType.DMA,
            pltpu.SemaphoreType.DMA((chunks,)),
        ],
        compiler_params=pltpu.CompilerParams(vmem_limit_bytes=GRANTS[2]),
        name="second",
    )(adv, packed, head, halo_n, halo_s, halo_e, halo_w, coef_n, coef_s, coef_e, coef_w,
      place, turned, base, w_in, whid, w_out)
    return out.reshape(lon, lat, ch)


def solution(mesh):
    spec = P(("member", "tx"), "ty", None)
    flat = P(("member", "tx"), "ty")
    return jax.shard_map(
        functools.partial(local, mesh.shape["tx"], mesh.shape["ty"]),
        mesh=mesh,
        in_specs=(spec, spec, flat, flat, P(), P(), P()),
        out_specs=spec,
        check_vma=False,
    )
```
